256 devices in a mesh: clip: 2 (over core), frame: 8 (over y, x_lo), band: 16 (over z, x_hi).
Axes of the slice: x: 4 (x_hi: 2, x_lo: 2; x = x_hi * 2 + x_lo), y: 4, z: 8, core: 2. Of those that a mesh axis runs over, the one named last changes fastest.
Arguments:
- latents: bfloat16 [4, 32, 64, 64, 320], P('clip', 'frame', 'band'), may hold values from -6 to 6
- spatial_kernel: bfloat16 [3, 3, 320, 320], replicated, may hold values from -0.109375 to 0.109375
- temporal_kernel: bfloat16 [3, 320, 320], replicated, may hold values from -0.1875 to 0.1875
- spatial_tangent: bfloat16 [3, 3, 320, 320], replicated, may hold values from -0.109375 to 0.109375
- temporal_tangent: bfloat16 [3, 320, 320], replicated, may hold values from -0.1875 to 0.1875
Outputs:
- curv_spatial: float32 [3, 3, 320, 320], replicated
- curv_temporal: float32 [3, 320, 320], replicated
The draws below stay inside these ranges and needn't reach their ends.
All inputs are finite; a program needn't handle non-finite values.
Results may differ from the reference program's by a relative error of at most 0.00075.
Values may be sent and summed in bfloat16 or wider, within the bound.
No kernel may reach another device: no remote copies, remote signals or barrier semaphores. Data moves between devices by JAX's collectives and lax.ppermute only.
A program may use at most 128 MiB of HBM per device.

```python
import jax
import jax.numpy as jnp
from jax import lax

C = 320
W = 64
CLIPS = 4
FRAMES = 32
H = 64


def shard_levels(rng, shape, split, low, top_value):
    level, own = 1.0, jax.random.fold_in(rng, 6)
    for dim, shards_of in split:
        draws = jnp.exp(jax.random.uniform(jax.random.fold_in(own, dim), (shards_of,), jnp.float32, low / len(split), top_value / len(split)))
        level = level * jnp.repeat(draws, shape[dim] // shards_of).reshape([-1 if axis == dim else 1 for axis in range(len(shape))])
    return level


def gaussian(rng, extent, scale, bound, cuts=(), kind=jnp.bfloat16):
    drawn = jax.random.normal(rng, extent, jnp.float32) * scale
    if len(cuts) > 0:
        drawn = shard_levels(rng, extent, cuts, -0.22, 0.18) * drawn
    return jnp.clip(drawn, min=-bound, max=bound).astype(kind)


def setup_inputs(seed: int = 0) -> dict:
    seeds = jax.random.split(jax.random.key(seed), 6)
    latents = gaussian(seeds[0], (CLIPS, FRAMES, H, W, C), 1.0, 6.0, ((0, 2), (1, 8), (2, 16)))
    spatial_kernel = gaussian(seeds[1], (3, 3, C, C), (9 * C) ** -0.5, 0.109375)
    temporal_kernel = gaussian(seeds[2], (3, C, C), (3 * C) ** -0.5, 0.1875)
    spatial_tangent = gaussian(seeds[3], (3, 3, C, C), (9 * C) ** -0.5, 0.109375)
    temporal_tangent = gaussian(seeds[4], (3, C, C), (3 * C) ** -0.5, 0.1875)
    return dict(latents=latents, spatial_kernel=spatial_kernel, temporal_kernel=temporal_kernel, spatial_tangent=spatial_tangent, temporal_tangent=temporal_tangent)


def flat_dot(left, right):
    shape = left.shape
    return jnp.dot(left.reshape(-1, shape[-1]), right, preferred_element_type=jnp.float32).reshape(shape[:-1] + (right.shape[-1],))


def outer_sum(left, right):
    return jnp.dot(left.reshape(-1, left.shape[-1]).T, right.reshape(-1, right.shape[-1]), preferred_element_type=jnp.float32)


def one_clip(carry, frames_in, spatial_kernel, temporal_kernel, spatial_tangent, temporal_tangent):
    chans = frames_in.shape[-1]
    nframe, rows, cols = frames_in.shape[0], frames_in.shape[1], frames_in.shape[2]
    padded = jnp.pad(frames_in, ((0, 0), (1, 1), (1, 1), (0, 0)))
    patches = jnp.concatenate([padded[:, i:i + rows, j:j + cols, :] for i in range(3) for j in range(3)], axis=-1)
    hidden = flat_dot(patches, spatial_kernel.reshape(9 * chans, chans))
    tangent = flat_dot(patches, spatial_tangent.reshape(9 * chans, chans))
    sig = jax.nn.sigmoid(hidden)
    slope = sig * (1.0 + hidden * (1.0 - sig))
    active = (hidden * sig).astype(jnp.bfloat16)
    active_dot = (slope * tangent).astype(jnp.bfloat16)
    act_pad = jnp.pad(active, ((1, 1), (0, 0), (0, 0), (0, 0)))
    dot_pad = jnp.pad(active_dot, ((1, 1), (0, 0), (0, 0), (0, 0)))
    cat_act = jnp.concatenate([act_pad[k:k + nframe] for k in range(3)], axis=-1)
    cat_dot = jnp.concatenate([dot_pad[k:k + nframe] for k in range(3)], axis=-1)
    resid = flat_dot(cat_act, temporal_tangent.reshape(3 * chans, chans)) + flat_dot(cat_dot, temporal_kernel.reshape(3 * chans, chans))
    residual = resid.astype(jnp.bfloat16)
    grad_t = outer_sum(cat_act, residual)
    res_pad = jnp.pad(residual, ((1, 1), (0, 0), (0, 0), (0, 0)))
    cat_res = jnp.concatenate([res_pad[2 - k:2 - k + nframe] for k in range(3)], axis=-1)
    back_w = jnp.concatenate([temporal_kernel[k].T for k in range(3)], axis=0)
    back = flat_dot(cat_res, back_w)
    hidden_bar = (slope * back).astype(jnp.bfloat16)
    grad_s = outer_sum(patches, hidden_bar)
    return (carry[0] + grad_s, carry[1] + grad_t)


def reference(latents, spatial_kernel, temporal_kernel, spatial_tangent, temporal_tangent):
    chans = latents.shape[-1]
    start = (jnp.zeros((9 * chans, chans), jnp.float32), jnp.zeros((3 * chans, chans), jnp.float32))

    def step(carry, frames_in):
        return one_clip(carry, frames_in, spatial_kernel, temporal_kernel, spatial_tangent, temporal_tangent), None

    totals, _ = lax.scan(step, start, latents)
    count = 1.0 * latents.shape[0] * latents.shape[1] * latents.shape[2] * latents.shape[3]
    curv_spatial = (totals[0] * ((9.0 * chans) ** 0.5 / count)).reshape(3, 3, chans, chans)
    curv_temporal = (totals[1] * ((3.0 * chans) ** 0.5 / count)).reshape(3, chans, chans)
    return curv_spatial, curv_temporal
```

```python
import jax
import jax.numpy as jnp
from jax import lax
from jax.experimental import pallas as pl
from jax.sharding import PartitionSpec as P


RING = ("frame", "band")
UNIT = 152
ROWS = 64 * UNIT


def place(y, x, z):
    return (2 * y + x % 2) * 16 + 2 * z + x // 2


def ring_perm(axis, step):
    pairs = []
    for y in range(4):
        for x in range(4):
            for z in range(8):
                if axis == "x":
                    to = place(y, (x + step) % 4, z)
                elif axis == "y":
                    to = place((y + step) % 4, x, z)
                else:
                    to = place(y, x, (z + step) % 8)
                pairs.append((place(y, x, z), to))
    return pairs


def steps_of(count):
    order = []
    for s in range(1, count // 2):
        order += [s, -s]
    return [count // 2] + order[::-1]


def pick(parts, index):
    return lax.dynamic_index_in_dim(parts, index, 0, keepdims=False)


def send_scatter(parts, axis, at):
    count = parts.shape[0]
    return [
        lax.ppermute(pick(parts, (at + s) % count), RING, ring_perm(axis, s))
        for s in steps_of(count)
    ]


def send_gather(mine, axis, count):
    return [lax.ppermute(mine, RING, ring_perm(axis, s)) for s in steps_of(count)]


def arrange(mine, got, at):
    count = len(got) + 1
    whole = jnp.zeros((count,) + mine.shape, mine.dtype)
    whole = lax.dynamic_update_index_in_dim(whole, mine, at, 0)
    for s, piece in zip(steps_of(count), got):
        whole = lax.dynamic_update_index_in_dim(whole, piece, (at - s) % count, 0)
    return whole


def reduce_all(buf):
    core = lax.axis_index("clip")
    frame = lax.axis_index("frame")
    band = lax.axis_index("band")
    y = frame // 2
    x = frame % 2 + 2 * (band % 2)
    z = band // 2
    halves = buf.reshape(2, 2, 4, 4, UNIT, 128)
    swap = [(0, 1), (1, 0)]
    half = pick(halves, core) + lax.ppermute(pick(halves, 1 - core), "clip", swap)
    a, b = half[0], half[1]
    ga, gb = send_scatter(a, "x", x), send_scatter(b, "y", y)
    a = sum(ga, pick(a, x))
    b = sum(gb, pick(b, y))
    ga, gb = send_scatter(a, "y", y), send_scatter(b, "x", x)
    a = sum(ga, pick(a, y))
    b = sum(gb, pick(b, x))
    both = jnp.concatenate([a, b, jnp.zeros((16, 128), a.dtype)]).reshape(8, 40, 128)
    mine = sum(send_scatter(both, "z", z), pick(both, z))
    both = arrange(mine, send_gather(mine, "z", 8), z).reshape(320, 128)
    a, b = both[:UNIT], both[UNIT : 2 * UNIT]
    ga, gb = send_gather(a, "y", 4), send_gather(b, "x", 4)
    a, b = arrange(a, ga, y), arrange(b, gb, x)
    ga, gb = send_gather(a, "x", 4), send_gather(b, "y", 4)
    a, b = arrange(a, ga, x), arrange(b, gb, y)
    half = jnp.stack([a, b])
    other = lax.ppermute(half, "clip", swap)
    return jnp.where(core == 0, jnp.stack([half, other]), jnp.stack([other, half])).reshape(ROWS, 128)


def pack_body(gs_ref, gt_ref, out_ref):
    out_ref[0:2880] = gs_ref[:, 0:128]
    out_ref[2880:3840] = gt_ref[:, 0:128]
    out_ref[3840:6720] = gs_ref[:, 128:256]
    out_ref[6720:7680] = gt_ref[:, 128:256]
    out_ref[7680:9600, 0:64] = gs_ref[0:1920, 256:320]
    out_ref[7680:8640, 64:128] = gs_ref[1920:2880, 256:320]
    out_ref[8640:9600, 64:128] = gt_ref[:, 256:320]
    out_ref[9600:ROWS] = jnp.zeros((ROWS - 9600, 128), jnp.float32)


def pack(gs, gt):
    return pl.pallas_call(pack_body, out_shape=jax.ShapeDtypeStruct((ROWS, 128), jnp.float32))(gs, gt)


def unpack(buf, scale_s, scale_t):
    def body(buf_ref, gs_ref, gt_ref):
        gs_ref[:, 0:128] = buf_ref[0:2880] * scale_s
        gt_ref[:, 0:128] = buf_ref[2880:3840] * scale_t
        gs_ref[:, 128:256] = buf_ref[3840:6720] * scale_s
        gt_ref[:, 128:256] = buf_ref[6720:7680] * scale_t
        gs_ref[0:1920, 256:320] = buf_ref[7680:9600, 0:64] * scale_s
        gs_ref[1920:2880, 256:320] = buf_ref[7680:8640, 64:128] * scale_s
        gt_ref[:, 256:320] = buf_ref[8640:9600, 64:128] * scale_t

    return pl.pallas_call(
        body,
        out_shape=(
            jax.ShapeDtypeStruct((2880, 320), jnp.float32),
            jax.ShapeDtypeStruct((960, 320), jnp.float32),
        ),
    )(buf)


def padded_2(cells, sides, width):
    for axis, dim in sides:
        count = lax.axis_size(axis)
        ends = count - 1
        head = lax.slice_in_dim(cells, 0, width, axis=dim)
        tail = lax.slice_in_dim(cells, cells.shape[dim] - width, cells.shape[dim], axis=dim)
        cells = jnp.concatenate(
            [
                lax.ppermute(tail, axis, [(i, (i + 1) % count) for i in range(ends)]),
                cells,
                lax.ppermute(head, axis, [((i + 1) % count, i) for i in range(ends)]),
            ],
            axis=dim,
        )
    return cells


def forward_frames(framed, temporal_kernel, temporal_tangent):
    chans = framed.shape[-1]
    nframe = framed.shape[2] - 2
    act_pad = framed[0]
    dot_pad = framed[1]
    cat_act = jnp.concatenate([act_pad[:, k : k + nframe] for k in range(3)], axis=-1)
    cat_dot = jnp.concatenate([dot_pad[:, k : k + nframe] for k in range(3)], axis=-1)
    resid = jnp.einsum(
        "abrwk,kd->abrwd",
        cat_act,
        temporal_tangent.reshape(3 * chans, chans),
        preferred_element_type=jnp.float32,
    )
    resid = resid + jnp.einsum(
        "abrwk,kd->abrwd",
        cat_dot,
        temporal_kernel.reshape(3 * chans, chans),
        preferred_element_type=jnp.float32,
    )
    residual = resid.astype(jnp.bfloat16)
    grad_t = jnp.einsum("abrwk,abrwd->kd", cat_act, residual, preferred_element_type=jnp.float32)
    return (residual, grad_t)


def backward_frames(res_pad, temporal_kernel):
    nframe = res_pad.shape[1] - 2
    cat_res = jnp.concatenate([res_pad[:, 2 - k : 2 - k + nframe] for k in range(3)], axis=-1)
    back_w = jnp.concatenate([temporal_kernel[k].T for k in range(3)], axis=0)
    return jnp.einsum("abrwk,kd->abrwd", cat_res, back_w, preferred_element_type=jnp.float32)


def per_device(latents, spatial_kernel, temporal_kernel, spatial_tangent, temporal_tangent):
    chans = latents.shape[-1]
    rows = latents.shape[2]
    cols = latents.shape[3]
    padded = padded_2(latents, (("band", 2),), 1)
    padded = jnp.pad(padded, ((0, 0), (0, 0), (0, 0), (1, 1), (0, 0)))
    patches = jnp.concatenate(
        [padded[:, :, i : i + rows, j : j + cols, :] for i in range(3) for j in range(3)], axis=-1
    )
    both_w = jnp.concatenate(
        [spatial_kernel.reshape(9 * chans, chans), spatial_tangent.reshape(9 * chans, chans)],
        axis=1,
    )
    before = jnp.einsum("abrwk,kd->abrwd", patches, both_w, preferred_element_type=jnp.float32)
    hidden = before[..., :chans]
    tangent = before[..., chans:]
    sig = jax.nn.sigmoid(hidden)
    slope = sig * (1.0 + hidden * (1.0 - sig))
    active = (hidden * sig).astype(jnp.bfloat16)
    active_dot = (slope * tangent).astype(jnp.bfloat16)
    stacked = jnp.stack([active, active_dot])
    framed = padded_2(stacked, (("frame", 2),), 1)
    residual, grad_t = forward_frames(framed, temporal_kernel, temporal_tangent)
    res_pad = padded_2(residual, (("frame", 1),), 1)
    back = backward_frames(res_pad, temporal_kernel)
    hidden_bar = (slope * back).astype(jnp.bfloat16)
    grad_s = jnp.einsum("abrwk,abrwd->kd", patches, hidden_bar, preferred_element_type=jnp.float32)
    total = reduce_all(pack(grad_s, grad_t))
    devices = lax.axis_size("clip") * lax.axis_size("frame") * lax.axis_size("band")
    count = 1.0 * latents.shape[0] * latents.shape[1] * rows * cols * devices
    curv_spatial, curv_temporal = unpack(total, (9.0 * chans) ** 0.5 / count, (3.0 * chans) ** 0.5 / count)
    curv_spatial = curv_spatial.reshape(3, 3, chans, chans)
    curv_temporal = curv_temporal.reshape(3, chans, chans)
    return (curv_spatial, curv_temporal)


def solution(mesh):
    in_specs = (P("clip", "frame", "band", None, None), P(), P(), P(), P())
    out_specs = (P(), P())
    return jax.shard_map(
        per_device, mesh=mesh, in_specs=in_specs, out_specs=out_specs, check_vma=False
    )
```

```python
import jax
import jax.numpy as jnp
from jax import lax
from jax.experimental import pallas as pl
from jax.experimental.pallas import tpu as pltpu
from jax.sharding import PartitionSpec as P

BF, F32 = jnp.bfloat16, jnp.float32
C = 320

RING = ("frame", "band")
UNIT = 152
ROWS = 64 * UNIT


def place(y, x, z):
    return (2 * y + x % 2) * 16 + 2 * z + x // 2


def ring_perm(axis, step):
    pairs = []
    for y in range(4):
        for x in range(4):
            for z in range(8):
                if axis == "x":
                    to = place(y, (x + step) % 4, z)
                elif axis == "y":
                    to = place((y + step) % 4, x, z)
                else:
                    to = place(y, x, (z + step) % 8)
                pairs.append((place(y, x, z), to))
    return pairs


def steps_of(count):
    order = []
    for s in range(1, count // 2):
        order += [s, -s]
    return [count // 2] + order[::-1]


def pick(parts, index):
    return lax.dynamic_index_in_dim(parts, index, 0, keepdims=False)


def send_scatter(parts, axis, at):
    count = parts.shape[0]
    return [
        lax.ppermute(pick(parts, (at + s) % count), RING, ring_perm(axis, s))
        for s in steps_of(count)
    ]


def send_gather(mine, axis, count):
    return [lax.ppermute(mine, RING, ring_perm(axis, s)) for s in steps_of(count)]


def arrange(mine, got, at):
    count = len(got) + 1
    whole = jnp.zeros((count,) + mine.shape, mine.dtype)
    whole = lax.dynamic_update_index_in_dim(whole, mine, at, 0)
    for s, piece in zip(steps_of(count), got):
        whole = lax.dynamic_update_index_in_dim(whole, piece, (at - s) % count, 0)
    return whole


def reduce_all(buf):
    core = lax.axis_index("clip")
    frame = lax.axis_index("frame")
    band = lax.axis_index("band")
    y = frame // 2
    x = frame % 2 + 2 * (band % 2)
    z = band // 2
    halves = buf.reshape(2, 2, 4, 4, UNIT, 128)
    swap = [(0, 1), (1, 0)]
    half = pick(halves, core) + lax.ppermute(pick(halves, 1 - core), "clip", swap)
    a, b = half[0], half[1]
    ga, gb = send_scatter(a, "x", x), send_scatter(b, "y", y)
    a = sum(ga, pick(a, x))
    b = sum(gb, pick(b, y))
    ga, gb = send_scatter(a, "y", y), send_scatter(b, "x", x)
    a = sum(ga, pick(a, y))
    b = sum(gb, pick(b, x))
    both = jnp.concatenate([a, b, jnp.zeros((16, 128), a.dtype)]).reshape(8, 40, 128)
    mine = sum(send_scatter(both, "z", z), pick(both, z))
    both = arrange(mine, send_gather(mine, "z", 8), z).reshape(320, 128)
    a, b = both[:UNIT], both[UNIT : 2 * UNIT]
    ga, gb = send_gather(a, "y", 4), send_gather(b, "x", 4)
    a, b = arrange(a, ga, y), arrange(b, gb, x)
    ga, gb = send_gather(a, "x", 4), send_gather(b, "y", 4)
    a, b = arrange(a, ga, x), arrange(b, gb, y)
    half = jnp.stack([a, b])
    other = lax.ppermute(half, "clip", swap)
    return half.reshape(ROWS // 2, 128), other.reshape(ROWS // 2, 128)


def sds(shape, dtype):
    return jax.ShapeDtypeStruct(shape, dtype)


def cost(flops, nbytes):
    return pl.CostEstimate(flops=flops, transcendentals=0, bytes_accessed=nbytes)


def dot(a, b):
    return jnp.dot(a, b, preferred_element_type=F32)


def dot_t(a, b):
    return lax.dot_general(a, b, (((0,), (0,)), ((), ())), preferred_element_type=F32)


def write_columns(row, out, at):
    wide = row.astype(F32)
    col = lax.broadcasted_iota(jnp.int32, (512, C), 0) & 63
    out[at, :, 0:C] = jnp.where(col == 0, 0.0, pltpu.roll(wide, 1, 0)).astype(BF)
    out[at, :, C : 2 * C] = row
    out[at, :, 2 * C : 3 * C] = jnp.where(col == 63, 0.0, pltpu.roll(wide, 511, 0)).astype(BF)


def inner_body(x_ref, w_ref, x3_ref, acc_ref):
    def build(r, carry):
        write_columns(x_ref[:, r].reshape(512, C), x3_ref, r)
        return carry

    lax.fori_loop(0, 4, build, 0)

    def taps(r, carry):
        acc_ref[r] = dot(x3_ref[r], w_ref[1])

        @pl.when(r > 0)
        def _():
            acc_ref[r] += dot(x3_ref[r - 1], w_ref[0])

        @pl.when(r < 3)
        def _():
            acc_ref[r] += dot(x3_ref[r + 1], w_ref[2])

        return carry

    lax.fori_loop(0, 4, taps, 0)


def inner(x, w):
    return pl.pallas_call(
        inner_body,
        out_shape=(sds((4, 512, 3 * C), BF), sds((4, 512, 768), F32)),
        cost_estimate=cost(6300000000, 20000000),
        name="inner",
    )(x, w)


def frame_rows(value, frame):
    return jnp.concatenate([value[frame * 64 : frame * 64 + 64], value[256 + frame * 64 : 320 + frame * 64]])


def outer_body(top_ref, bot_ref, w_ref, acc_ref, tw_ref, xt_ref, xb_ref, slope_ref, ad_ref, pn_ref, pp_ref, work_ref):
    write_columns(top_ref[...].reshape(512, C), xt_ref, 0)
    write_columns(bot_ref[...].reshape(512, C), xb_ref, 0)
    work_ref[0] = dot(xt_ref[0], w_ref[0])
    work_ref[1] = jnp.zeros((512, 768), F32)
    work_ref[2] = jnp.zeros((512, 768), F32)
    work_ref[3] = dot(xb_ref[0], w_ref[2])

    def one(r, carry):
        hidden = acc_ref[r, :, 0:C] + work_ref[r, :, 0:C]
        tangent = acc_ref[r, :, 384 : 384 + C] + work_ref[r, :, 384 : 384 + C]
        sig = jax.nn.sigmoid(hidden)
        slope = sig * (1.0 + hidden * (1.0 - sig))
        slope_ref[r] = slope
        ad_ref[r, :, 0:C] = (hidden * sig).astype(BF)
        ad_ref[r, :, C:384] = jnp.zeros((512, 64), BF)
        ad_ref[r, :, 384 : 384 + C] = (slope * tangent).astype(BF)
        ad_ref[r, :, 384 + C : 768] = jnp.zeros((512, 64), BF)
        last = frame_rows(ad_ref[r], 3)
        first = frame_rows(ad_ref[r], 0)
        pn_ref[r] = dot(last, tw_ref[:, 0:C]).astype(BF)
        pp_ref[r] = dot(first, tw_ref[:, 2 * C : 3 * C]).astype(BF)
        return carry

    lax.fori_loop(0, 4, one, 0)


def outer(top, bot, w, acc, tw):
    return pl.pallas_call(
        outer_body,
        out_shape=(
            sds((1, 512, 3 * C), BF),
            sds((1, 512, 3 * C), BF),
            sds((4, 512, C), F32),
            sds((4, 512, 768), BF),
            sds((4, 128, C), BF),
            sds((4, 128, C), BF),
        ),
        scratch_shapes=[pltpu.VMEM((4, 512, 768), F32)],
        cost_estimate=cost(1500000000, 25000000),
        name="outer",
    )(top, bot, w, acc, tw)


def own_res_body(ad_ref, tw_ref, res_ref, u_ref):
    def one(r, carry):
        u_ref[...] = dot(ad_ref[r], tw_ref[...])
        for clip in range(2):
            o = 256 * clip
            res_ref[r, o : o + 256] = u_ref[o : o + 256, C : 2 * C]
            res_ref[r, o + 64 : o + 256] += u_ref[o : o + 192, 0:C]
            res_ref[r, o : o + 192] += u_ref[o + 64 : o + 256, 2 * C : 3 * C]
        return carry

    lax.fori_loop(0, 4, one, 0)


def own_res(ad, tw):
    return pl.pallas_call(
        own_res_body,
        out_shape=sds((4, 512, C), F32),
        scratch_shapes=[pltpu.VMEM((512, 3 * C), F32)],
        cost_estimate=cost(3000000000, 7000000),
        name="own_res",
    )(ad, tw)


def close_body(part_ref, before_ref, after_ref, res_ref, first_ref, last_ref):
    for clip in range(2):
        o, h = 256 * clip, 64 * clip
        first = (part_ref[:, o : o + 64] + before_ref[:, h : h + 64].astype(F32)).astype(BF)
        last = (part_ref[:, o + 192 : o + 256] + after_ref[:, h : h + 64].astype(F32)).astype(BF)
        res_ref[:, o : o + 64] = first
        res_ref[:, o + 64 : o + 192] = part_ref[:, o + 64 : o + 192].astype(BF)
        res_ref[:, o + 192 : o + 256] = last
        first_ref[:, h : h + 64] = first
        last_ref[:, h : h + 64] = last


def close(part, before, after):
    return pl.pallas_call(
        close_body,
        out_shape=(sds((4, 512, C), BF), sds((4, 128, C), BF), sds((4, 128, C), BF)),
        cost_estimate=cost(2000000, 5000000),
        name="close",
    )(part, before, after)


def own_back_body(res_ref, ad_ref, tkt_ref, back_ref, gt_ref, r3_ref):
    gap = jnp.zeros((64, C), BF)

    def one(r, carry):
        for clip in range(2):
            o = 256 * clip
            r3_ref[r, o : o + 192, 0:C] = res_ref[r, o + 64 : o + 256]
            r3_ref[r, o + 192 : o + 256, 0:C] = gap
            r3_ref[r, o : o + 256, C : 2 * C] = res_ref[r, o : o + 256]
            r3_ref[r, o : o + 64, 2 * C : 3 * C] = gap
            r3_ref[r, o + 64 : o + 256, 2 * C : 3 * C] = res_ref[r, o : o + 192]
        back_ref[r] = dot(r3_ref[r], tkt_ref[...])
        return carry

    lax.fori_loop(0, 4, one, 0)
    gt_ref[...] = dot_t(ad_ref[:, :, 0:C].reshape(2048, C), r3_ref[...].reshape(2048, 3 * C))


def own_back(res, ad, tkt):
    return pl.pallas_call(
        own_back_body,
        out_shape=(sds((4, 512, C), F32), sds((C, 3 * C), F32)),
        scratch_shapes=[pltpu.VMEM((4, 512, 3 * C), BF)],
        cost_estimate=cost(3000000000, 9000000),
        name="own_back",
    )(res, ad, tkt)


def put_columns(out_ref, start, value):
    done = 0
    while done < value.shape[1]:
        j, lane = (start + done) // 128, (start + done) % 128
        n = min(128 - lane, value.shape[1] - done)
        out_ref[j * C : (j + 1) * C, lane : lane + n] = value[:, done : done + n]
        done += n


def grads_body(before_ref, after_ref, back_ref, slope_ref, ad_ref, tkt_ref, gt_ref, x3_ref, xt_ref, xb_ref, out_ref, x6_ref, hb_ref, halo_ref):
    x6_ref[0] = xt_ref[0]
    x6_ref[1:5] = x3_ref[...]
    x6_ref[5] = xb_ref[0]
    before = before_ref[...].reshape(512, C)
    after = after_ref[...].reshape(512, C)
    halo_ref[0] = dot(before, tkt_ref[2 * C : 3 * C]).reshape(4, 128, C)
    halo_ref[1] = dot(after, tkt_ref[0:C]).reshape(4, 128, C)
    for clip in range(2):
        o, h = 256 * clip, 64 * clip
        first, last = slice(o, o + 64), slice(o + 192, o + 256)
        mid, edge = slice(o + 64, o + 192), slice(h, h + 64)
        hb_ref[:, first] = (slope_ref[:, first] * (back_ref[:, first] + halo_ref[0, :, edge])).astype(BF)
        hb_ref[:, mid] = (slope_ref[:, mid] * back_ref[:, mid]).astype(BF)
        hb_ref[:, last] = (slope_ref[:, last] * (back_ref[:, last] + halo_ref[1, :, edge])).astype(BF)
    act_last = jnp.concatenate([frame_rows(ad_ref[r], 3)[:, 0:C] for r in range(4)])
    act_first = jnp.concatenate([frame_rows(ad_ref[r], 0)[:, 0:C] for r in range(4)])
    put_columns(out_ref, 9 * C, gt_ref[:, 0:C] + dot_t(act_last, after))
    put_columns(out_ref, 10 * C, gt_ref[:, C : 2 * C])
    put_columns(out_ref, 11 * C, gt_ref[:, 2 * C : 3 * C] + dot_t(act_first, before))
    hbt = hb_ref[...].reshape(2048, C).T
    for i in range(3):
        put_columns(out_ref, 3 * C * i, dot(hbt, x6_ref[i : i + 4].reshape(2048, 3 * C)))
    out_ref[30 * C : ROWS] = jnp.zeros((ROWS - 30 * C, 128), F32)


def grads(before, after, back, slope, ad, tkt, gt, x3, xt, xb):
    return pl.pallas_call(
        grads_body,
        out_shape=sds((ROWS, 128), F32),
        scratch_shapes=[
            pltpu.VMEM((6, 512, 3 * C), BF),
            pltpu.VMEM((4, 512, C), BF),
            pltpu.VMEM((2, 4, 128, C), F32),
        ],
        cost_estimate=cost(4500000000, 20000000),
        name="grads",
    )(before, after, back, slope, ad, tkt, gt, x3, xt, xb)


def unpack(core, own, other, scale_s, scale_t):
    def body(core_ref, own_ref, other_ref, gs_ref, gt_ref, buf_ref):
        at = core_ref[0]
        half = ROWS // 2
        buf_ref[pl.ds(at * half, half)] = own_ref[...]
        buf_ref[pl.ds((1 - at) * half, half)] = other_ref[...]
        for j in range(22):
            gs_ref[j * 128 : j * 128 + 128] = buf_ref[j * C : (j + 1) * C].T * scale_s
        gs_ref[22 * 128 : 9 * C] = buf_ref[22 * C : 23 * C].T[0:64] * scale_s
        for k in range(3):
            done = 0
            while done < C:
                j, lane = ((9 + k) * C + done) // 128, ((9 + k) * C + done) % 128
                n = min(128 - lane, C - done)
                gt_ref[k, :, done : done + n] = buf_ref[j * C : (j + 1) * C, lane : lane + n] * scale_t
                done += n

    return pl.pallas_call(
        body,
        out_shape=(sds((9 * C, C), F32), sds((3, C, C), F32)),
        in_specs=[
            pl.BlockSpec(memory_space=pltpu.SMEM),
            pl.BlockSpec(memory_space=pltpu.VMEM),
            pl.BlockSpec(memory_space=pltpu.VMEM),
        ],
        scratch_shapes=[pltpu.VMEM((ROWS, 128), F32)],
        cost_estimate=cost(2000000, 10000000),
        name="unpack",
    )(core, own, other)


def to_next(value, axis):
    n = lax.axis_size(axis)
    return lax.ppermute(value, axis, [(i, i + 1) for i in range(n - 1)])


def to_prev(value, axis):
    n = lax.axis_size(axis)
    return lax.ppermute(value, axis, [(i + 1, i) for i in range(n - 1)])


def per_device(latents, spatial_kernel, temporal_kernel, spatial_tangent, temporal_tangent):
    x = latents.reshape(8, 4, 64, C)
    top = to_next(x[:, 3], "band")
    bot = to_prev(x[:, 0], "band")
    gap = jnp.zeros((3, 3 * C, 64), BF)
    w = jnp.concatenate(
        [spatial_kernel.reshape(3, 3 * C, C), gap, spatial_tangent.reshape(3, 3 * C, C), gap], axis=2
    )
    zero = jnp.zeros((64, 3 * C), BF)
    tw = jnp.concatenate(
        [
            temporal_tangent.transpose(1, 0, 2).reshape(C, 3 * C),
            zero,
            temporal_kernel.transpose(1, 0, 2).reshape(C, 3 * C),
            zero,
        ],
        axis=0,
    )
    tkt = temporal_kernel.transpose(0, 2, 1).reshape(3 * C, C)
    x3, acc = inner(x, w)
    xt, xb, slope, ad, p_next, p_prev = outer(top, bot, w, acc, tw)
    before, after = to_next(p_next, "frame"), to_prev(p_prev, "frame")
    res, first, last = close(own_res(ad, tw), before, after)
    before, after = to_next(last, "frame"), to_prev(first, "frame")
    back, gt = own_back(res, ad, tkt)
    buf = grads(before, after, back, slope, ad, tkt, gt, x3, xt, xb)
    own, other = reduce_all(buf)
    count = 1.0 * latents.shape[0] * latents.shape[1] * latents.shape[2] * latents.shape[3]
    count = count * lax.axis_size("clip") * lax.axis_size("frame") * lax.axis_size("band")
    core = lax.axis_index("clip").astype(jnp.int32).reshape(1)
    gs, gt = unpack(core, own, other, (9.0 * C) ** 0.5 / count, (3.0 * C) ** 0.5 / count)
    return gs.reshape(3, 3, C, C), gt


def solution(mesh):
    in_specs = (P("clip", "frame", "band", None, None), P(), P(), P(), P())
    return jax.shard_map(
        per_device, mesh=mesh, in_specs=in_specs, out_specs=(P(), P()), check_vma=False
    )
```

```python
import jax
import jax.numpy as jnp
from jax import lax
from jax.experimental import pallas as pl
from jax.experimental.pallas import tpu as pltpu
from jax.sharding import PartitionSpec as P

BF, F32 = jnp.bfloat16, jnp.float32
C = 320

RING = ("frame", "band")
UNIT = 152
ROWS = 64 * UNIT


def place(y, x, z):
    return (2 * y + x % 2) * 16 + 2 * z + x // 2


def ring_perm(axis, step):
    pairs = []
    for y in range(4):
        for x in range(4):
            for z in range(8):
                if axis == "x":
                    to = place(y, (x + step) % 4, z)
                else:
                    to = place((y + step) % 4, x, z)
                pairs.append((place(y, x, z), to))
    return pairs


def flip_perm(bit):
    return [
        (place(y, x, z), place(y, x, z ^ (1 << bit)))
        for y in range(4)
        for x in range(4)
        for z in range(8)
    ]


def steps_of(count):
    order = []
    for s in range(1, count // 2):
        order += [s, -s]
    return [count // 2] + order[::-1]


def pick(parts, index):
    return lax.dynamic_index_in_dim(parts, index, 0, keepdims=False)


def send_scatter(parts, axis, at):
    count = parts.shape[0]
    return [
        lax.ppermute(pick(parts, (at + s) % count), RING, ring_perm(axis, s))
        for s in steps_of(count)
    ]


def send_gather(mine, axis, count):
    return [lax.ppermute(mine, RING, ring_perm(axis, s)) for s in steps_of(count)]


def arrange(mine, got, at):
    count = len(got) + 1
    whole = jnp.zeros((count,) + mine.shape, mine.dtype)
    whole = lax.dynamic_update_index_in_dim(whole, mine, at, 0)
    for s, piece in zip(steps_of(count), got):
        whole = lax.dynamic_update_index_in_dim(whole, piece, (at - s) % count, 0)
    return whole


def reduce_all(buf):
    core = lax.axis_index("clip")
    frame = lax.axis_index("frame")
    band = lax.axis_index("band")
    y = frame // 2
    x = frame % 2 + 2 * (band % 2)
    z = band // 2
    halves = buf.reshape(2, 2, 4, 4, UNIT, 128)
    swap = [(0, 1), (1, 0)]
    half = pick(halves, core) + lax.ppermute(pick(halves, 1 - core), "clip", swap)
    a, b = half[0], half[1]
    ga, gb = send_scatter(a, "x", x), send_scatter(b, "y", y)
    a = sum(ga, pick(a, x))
    b = sum(gb, pick(b, y))
    ga, gb = send_scatter(a, "y", y), send_scatter(b, "x", x)
    a = sum(ga, pick(a, y))
    b = sum(gb, pick(b, x))
    both = jnp.concatenate([a, b, jnp.zeros((16, 128), a.dtype)])
    for bit in range(3):
        parts = both.reshape(2, -1, 128)
        side = (z >> bit) & 1
        both = pick(parts, side) + lax.ppermute(pick(parts, 1 - side), RING, flip_perm(bit))
    for bit in (2, 1, 0):
        other = lax.ppermute(both, RING, flip_perm(bit))
        low = (z >> bit) & 1 == 0
        both = jnp.concatenate([jnp.where(low, both, other), jnp.where(low, other, both)])
    a, b = both[:UNIT], both[UNIT : 2 * UNIT]
    ga, gb = send_gather(a, "y", 4), send_gather(b, "x", 4)
    a, b = arrange(a, ga, y), arrange(b, gb, x)
    ga, gb = send_gather(a, "x", 4), send_gather(b, "y", 4)
    a, b = arrange(a, ga, x), arrange(b, gb, y)
    half = jnp.stack([a, b])
    other = lax.ppermute(half, "clip", swap)
    return half.reshape(ROWS // 2, 128), other.reshape(ROWS // 2, 128)


def sds(shape, dtype):
    return jax.ShapeDtypeStruct(shape, dtype)


def cost(flops, nbytes):
    return pl.CostEstimate(flops=flops, transcendentals=0, bytes_accessed=nbytes)


def local(body, name, flops, out_shape, args, scratch=(), grant=16):
    spec = pl.BlockSpec(memory_space=pltpu.VMEM)
    many = isinstance(out_shape, tuple)
    return pl.pallas_call(
        body,
        out_shape=out_shape,
        in_specs=[spec] * len(args),
        out_specs=tuple(spec for _ in out_shape) if many else spec,
        scratch_shapes=list(scratch),
        compiler_params=pltpu.CompilerParams(vmem_limit_bytes=grant << 20),
        cost_estimate=cost(flops, 1000000),
        name=name,
    )(*args)


def dot(a, b):
    return jnp.dot(a, b, preferred_element_type=F32)


def dot_t(a, b):
    return lax.dot_general(a, b, (((0,), (0,)), ((), ())), preferred_element_type=F32)


def write_columns(row, out, at):
    wide = row.astype(F32)
    col = lax.broadcasted_iota(jnp.int32, (512, C), 0) & 63
    out[at, :, 0:C] = jnp.where(col == 0, 0.0, pltpu.roll(wide, 1, 0)).astype(BF)
    out[at, :, C : 2 * C] = row
    out[at, :, 2 * C : 3 * C] = jnp.where(col == 63, 0.0, pltpu.roll(wide, 511, 0)).astype(BF)


def inner_body(x_ref, w_ref, x3_ref, acc_ref):
    def build(r, carry):
        write_columns(x_ref[:, r].reshape(512, C), x3_ref, r)
        return carry

    lax.fori_loop(0, 4, build, 0)

    def taps(r, carry):
        acc_ref[r] = dot(x3_ref[r], w_ref[1])

        @pl.when(r > 0)
        def _():
            acc_ref[r] += dot(x3_ref[r - 1], w_ref[0])

        @pl.when(r < 3)
        def _():
            acc_ref[r] += dot(x3_ref[r + 1], w_ref[2])

        return carry

    lax.fori_loop(0, 4, taps, 0)


def inner(x, w):
    shapes = (sds((4, 512, 3 * C), BF), sds((4, 512, 768), F32))
    return local(inner_body, "inner", 6300000000, shapes, (x, w))


def frame_rows(value, frame):
    return jnp.concatenate([value[frame * 64 : frame * 64 + 64], value[256 + frame * 64 : 320 + frame * 64]])


def outer_body(top_ref, bot_ref, w_ref, acc_ref, tw_ref, xt_ref, xb_ref, slope_ref, ad_ref, pn_ref, pp_ref, work_ref):
    write_columns(top_ref[...].reshape(512, C), xt_ref, 0)
    write_columns(bot_ref[...].reshape(512, C), xb_ref, 0)
    work_ref[0] = dot(xt_ref[0], w_ref[0])
    work_ref[1] = jnp.zeros((512, 768), F32)
    work_ref[2] = jnp.zeros((512, 768), F32)
    work_ref[3] = dot(xb_ref[0], w_ref[2])

    def one(r, carry):
        hidden = acc_ref[r, :, 0:C] + work_ref[r, :, 0:C]
        tangent = acc_ref[r, :, 384 : 384 + C] + work_ref[r, :, 384 : 384 + C]
        sig = jax.nn.sigmoid(hidden)
        slope = sig * (1.0 + hidden * (1.0 - sig))
        slope_ref[r] = slope
        ad_ref[r, :, 0:C] = (hidden * sig).astype(BF)
        ad_ref[r, :, C:384] = jnp.zeros((512, 64), BF)
        ad_ref[r, :, 384 : 384 + C] = (slope * tangent).astype(BF)
        ad_ref[r, :, 384 + C : 768] = jnp.zeros((512, 64), BF)
        last = frame_rows(ad_ref[r], 3)
        first = frame_rows(ad_ref[r], 0)
        pn_ref[r] = dot(last, tw_ref[:, 0:C]).astype(BF)
        pp_ref[r] = dot(first, tw_ref[:, 2 * C : 3 * C]).astype(BF)
        return carry

    lax.fori_loop(0, 4, one, 0)


def outer(top, bot, w, acc, tw):
    shapes = (
        sds((1, 512, 3 * C), BF),
        sds((1, 512, 3 * C), BF),
        sds((4, 512, C), F32),
        sds((4, 512, 768), BF),
        sds((4, 128, C), BF),
        sds((4, 128, C), BF),
    )
    scratch = (pltpu.VMEM((4, 512, 768), F32),)
    return local(outer_body, "outer", 1500000000, shapes, (top, bot, w, acc, tw), scratch, 24)


def own_res_body(ad_ref, tw_ref, res_ref, u_ref):
    def one(r, carry):
        u_ref[...] = dot(ad_ref[r], tw_ref[...])
        for clip in range(2):
            o = 256 * clip
            res_ref[r, o : o + 256] = u_ref[o : o + 256, C : 2 * C]
            res_ref[r, o + 64 : o + 256] += u_ref[o : o + 192, 0:C]
            res_ref[r, o : o + 192] += u_ref[o + 64 : o + 256, 2 * C : 3 * C]
        return carry

    lax.fori_loop(0, 4, one, 0)


def own_res(ad, tw):
    scratch = (pltpu.VMEM((512, 3 * C), F32),)
    return local(own_res_body, "own_res", 3000000000, sds((4, 512, C), F32), (ad, tw), scratch)


def close_body(part_ref, before_ref, after_ref, res_ref, first_ref, last_ref):
    for clip in range(2):
        o, h = 256 * clip, 64 * clip
        first = (part_ref[:, o : o + 64] + before_ref[:, h : h + 64].astype(F32)).astype(BF)
        last = (part_ref[:, o + 192 : o + 256] + after_ref[:, h : h + 64].astype(F32)).astype(BF)
        res_ref[:, o : o + 64] = first
        res_ref[:, o + 64 : o + 192] = part_ref[:, o + 64 : o + 192].astype(BF)
        res_ref[:, o + 192 : o + 256] = last
        first_ref[:, h : h + 64] = first
        last_ref[:, h : h + 64] = last


def close(part, before, after):
    shapes = (sds((4, 512, C), BF), sds((4, 128, C), BF), sds((4, 128, C), BF))
    return local(close_body, "close", 2000000, shapes, (part, before, after))


def own_back_body(res_ref, ad_ref, tkt_ref, back_ref, gt_ref, r3_ref):
    gap = jnp.zeros((64, C), BF)

    def one(r, carry):
        for clip in range(2):
            o = 256 * clip
            r3_ref[r, o : o + 192, 0:C] = res_ref[r, o + 64 : o + 256]
            r3_ref[r, o + 192 : o + 256, 0:C] = gap
            r3_ref[r, o : o + 256, C : 2 * C] = res_ref[r, o : o + 256]
            r3_ref[r, o : o + 64, 2 * C : 3 * C] = gap
            r3_ref[r, o + 64 : o + 256, 2 * C : 3 * C] = res_ref[r, o : o + 192]
        back_ref[r] = dot(r3_ref[r], tkt_ref[...])
        return carry

    lax.fori_loop(0, 4, one, 0)
    gt_ref[...] = dot_t(ad_ref[:, :, 0:C].reshape(2048, C), r3_ref[...].reshape(2048, 3 * C))


def own_back(res, ad, tkt):
    shapes = (sds((4, 512, C), F32), sds((C, 3 * C), F32))
    scratch = (pltpu.VMEM((4, 512, 3 * C), BF),)
    return local(own_back_body, "own_back", 3000000000, shapes, (res, ad, tkt), scratch, 24)


def put_columns(out_ref, start, value):
    done = 0
    while done < value.shape[1]:
        j, lane = (start + done) // 128, (start + done) % 128
        n = min(128 - lane, value.shape[1] - done)
        out_ref[j * C : (j + 1) * C, lane : lane + n] = value[:, done : done + n]
        done += n


def grads_body(before_ref, after_ref, back_ref, slope_ref, ad_ref, tkt_ref, gt_ref, x3_ref, xt_ref, xb_ref, out_ref, x6_ref, hb_ref, halo_ref):
    x6_ref[0] = xt_ref[0]
    x6_ref[1:5] = x3_ref[...]
    x6_ref[5] = xb_ref[0]
    before = before_ref[...].reshape(512, C)
    after = after_ref[...].reshape(512, C)
    halo_ref[0] = dot(before, tkt_ref[2 * C : 3 * C]).reshape(4, 128, C)
    halo_ref[1] = dot(after, tkt_ref[0:C]).reshape(4, 128, C)
    for clip in range(2):
        o, h = 256 * clip, 64 * clip
        first, last = slice(o, o + 64), slice(o + 192, o + 256)
        mid, edge = slice(o + 64, o + 192), slice(h, h + 64)
        hb_ref[:, first] = (slope_ref[:, first] * (back_ref[:, first] + halo_ref[0, :, edge])).astype(BF)
        hb_ref[:, mid] = (slope_ref[:, mid] * back_ref[:, mid]).astype(BF)
        hb_ref[:, last] = (slope_ref[:, last] * (back_ref[:, last] + halo_ref[1, :, edge])).astype(BF)
    act_last = jnp.concatenate([frame_rows(ad_ref[r], 3)[:, 0:C] for r in range(4)])
    act_first = jnp.concatenate([frame_rows(ad_ref[r], 0)[:, 0:C] for r in range(4)])
    put_columns(out_ref, 9 * C, gt_ref[:, 0:C] + dot_t(act_last, after))
    put_columns(out_ref, 10 * C, gt_ref[:, C : 2 * C])
    put_columns(out_ref, 11 * C, gt_ref[:, 2 * C : 3 * C] + dot_t(act_first, before))
    hbt = hb_ref[...].reshape(2048, C).T
    for i in range(3):
        put_columns(out_ref, 3 * C * i, dot(hbt, x6_ref[i : i + 4].reshape(2048, 3 * C)))
    out_ref[30 * C : ROWS] = jnp.zeros((ROWS - 30 * C, 128), F32)


def grads(*args):
    scratch = (
        pltpu.VMEM((6, 512, 3 * C), BF),
        pltpu.VMEM((4, 512, C), BF),
        pltpu.VMEM((2, 4, 128, C), F32),
    )
    return local(grads_body, "grads", 4500000000, sds((ROWS, 128), F32), args, scratch, 32)


def unpack(core, own, other, scale_s, scale_t):
    def body(core_ref, own_ref, other_ref, gs_ref, gt_ref, buf_ref):
        at = core_ref[0]
        half = ROWS // 2
        buf_ref[pl.ds(at * half, half)] = own_ref[...]
        buf_ref[pl.ds((1 - at) * half, half)] = other_ref[...]
        for j in range(22):
            gs_ref[j * 128 : j * 128 + 128] = buf_ref[j * C : (j + 1) * C].T * scale_s
        gs_ref[22 * 128 : 9 * C] = buf_ref[22 * C : 23 * C].T[0:64] * scale_s
        for k in range(3):
            done = 0
            while done < C:
                j, lane = ((9 + k) * C + done) // 128, ((9 + k) * C + done) % 128
                n = min(128 - lane, C - done)
                gt_ref[k, :, done : done + n] = buf_ref[j * C : (j + 1) * C, lane : lane + n] * scale_t
                done += n

    return pl.pallas_call(
        body,
        out_shape=(sds((9 * C, C), F32), sds((3, C, C), F32)),
        compiler_params=pltpu.CompilerParams(vmem_limit_bytes=32 << 20),
        in_specs=[
            pl.BlockSpec(memory_space=pltpu.SMEM),
            pl.BlockSpec(memory_space=pltpu.VMEM),
            pl.BlockSpec(memory_space=pltpu.VMEM),
        ],
        scratch_shapes=[pltpu.VMEM((ROWS, 128), F32)],
        cost_estimate=cost(2000000, 10000000),
        name="unpack",
    )(core, own, other)


def to_next(value, axis):
    n = lax.axis_size(axis)
    return lax.ppermute(value, axis, [(i, i + 1) for i in range(n - 1)])


def to_prev(value, axis):
    n = lax.axis_size(axis)
    return lax.ppermute(value, axis, [(i + 1, i) for i in range(n - 1)])


def per_device(latents, spatial_kernel, temporal_kernel, spatial_tangent, temporal_tangent):
    x = latents.reshape(8, 4, 64, C)
    top = to_next(x[:, 3], "band")
    bot = to_prev(x[:, 0], "band")
    gap = jnp.zeros((3, 3 * C, 64), BF)
    w = jnp.concatenate(
        [spatial_kernel.reshape(3, 3 * C, C), gap, spatial_tangent.reshape(3, 3 * C, C), gap], axis=2
    )
    zero = jnp.zeros((64, 3 * C), BF)
    tw = jnp.concatenate(
        [
            temporal_tangent.transpose(1, 0, 2).reshape(C, 3 * C),
            zero,
            temporal_kernel.transpose(1, 0, 2).reshape(C, 3 * C),
            zero,
        ],
        axis=0,
    )
    tkt = temporal_kernel.transpose(0, 2, 1).reshape(3 * C, C)
    x3, acc = inner(x, w)
    xt, xb, slope, ad, p_next, p_prev = outer(top, bot, w, acc, tw)
    before, after = to_next(p_next, "frame"), to_prev(p_prev, "frame")
    res, first, last = close(own_res(ad, tw), before, after)
    before, after = to_next(last, "frame"), to_prev(first, "frame")
    back, gt = own_back(res, ad, tkt)
    buf = grads(before, after, back, slope, ad, tkt, gt, x3, xt, xb)
    own, other = reduce_all(buf)
    count = 1.0 * latents.shape[0] * latents.shape[1] * latents.shape[2] * latents.shape[3]
    count = count * lax.axis_size("clip") * lax.axis_size("frame") * lax.axis_size("band")
    core = lax.axis_index("clip").astype(jnp.int32).reshape(1)
    gs, gt = unpack(core, own, other, (9.0 * C) ** 0.5 / count, (3.0 * C) ** 0.5 / count)
    return gs.reshape(3, 3, C, C), gt


def solution(mesh):
    in_specs = (P("clip", "frame", "band", None, None), P(), P(), P(), P())
    return jax.shard_map(
        per_device, mesh=mesh, in_specs=in_specs, out_specs=(P(), P()), check_vma=False
    )
```

```python
import jax
import jax.numpy as jnp
from jax import lax
from jax.experimental import pallas as pl
from jax.experimental.pallas import tpu as pltpu
from jax.sharding import PartitionSpec as P

BF, F32 = jnp.bfloat16, jnp.float32
C = 320

RING = ("frame", "band")
UNIT = 152
ROWS = 64 * UNIT


def place(y, x, z):
    return (2 * y + x % 2) * 16 + 2 * z + x // 2


def ring_perm(axis, step):
    pairs = []
    for y in range(4):
        for x in range(4):
            for z in range(8):
                if axis == "x":
                    to = place(y, (x + step) % 4, z)
                elif axis == "y":
                    to = place((y + step) % 4, x, z)
                else:
                    to = place(y, x, (z + step) % 8)
                pairs.append((place(y, x, z), to))
    return pairs


def steps_of(count):
    order = []
    for s in range(1, count // 2):
        order += [s, -s]
    return [count // 2] + order[::-1]


def pick(parts, index):
    return lax.dynamic_index_in_dim(parts, index, 0, keepdims=False)


def send_scatter(parts, axis, at):
    count = parts.shape[0]
    return [
        lax.ppermute(pick(parts, (at + s) % count), RING, ring_perm(axis, s))
        for s in steps_of(count)
    ]


def send_gather(mine, axis, count):
    return [lax.ppermute(mine, RING, ring_perm(axis, s)) for s in steps_of(count)]


def arrange(mine, got, at):
    count = len(got) + 1
    whole = jnp.zeros((count,) + mine.shape, mine.dtype)
    whole = lax.dynamic_update_index_in_dim(whole, mine, at, 0)
    for s, piece in zip(steps_of(count), got):
        whole = lax.dynamic_update_index_in_dim(whole, piece, (at - s) % count, 0)
    return whole


def reduce_all(send, keep):
    frame = lax.axis_index("frame")
    band = lax.axis_index("band")
    y = frame // 2
    x = frame % 2 + 2 * (band % 2)
    z = band // 2
    swap = [(0, 1), (1, 0)]
    half = (keep + lax.ppermute(send, "clip", swap)).reshape(2, 4, 4, UNIT, 128)
    a, b = half[0], half[1]
    ga, gb = send_scatter(a, "x", x), send_scatter(b, "y", y)
    a = sum(ga, pick(a, x))
    b = sum(gb, pick(b, y))
    ga, gb = send_scatter(a, "y", y), send_scatter(b, "x", x)
    a = sum(ga, pick(a, y))
    b = sum(gb, pick(b, x))
    both = jnp.concatenate([a, b, jnp.zeros((16, 128), a.dtype)])
    parts = both.reshape(2, 160, 128)
    side = z & 1
    pair = [(place(y, x, z), place(y, x, z ^ 1)) for y in range(4) for x in range(4) for z in range(8)]
    both = pick(parts, side) + lax.ppermute(pick(parts, 1 - side), RING, pair)
    far, near, back = [lax.ppermute(both, RING, ring_perm("z", s)) for s in (4, 2, -2)]
    both = (both + far) + (near + back)
    other = lax.ppermute(both, RING, pair)
    low = side == 0
    both = jnp.concatenate([jnp.where(low, both, other), jnp.where(low, other, both)])
    a, b = both[:UNIT], both[UNIT : 2 * UNIT]
    ga, gb = send_gather(a, "y", 4), send_gather(b, "x", 4)
    a, b = arrange(a, ga, y), arrange(b, gb, x)
    ga, gb = send_gather(a, "x", 4), send_gather(b, "y", 4)
    a, b = arrange(a, ga, x), arrange(b, gb, y)
    half = jnp.stack([a, b])
    other = lax.ppermute(half, "clip", swap)
    return half.reshape(ROWS // 2, 128), other.reshape(ROWS // 2, 128)


def sds(shape, dtype):
    return jax.ShapeDtypeStruct(shape, dtype)


def cost(flops, nbytes):
    return pl.CostEstimate(flops=flops, transcendentals=0, bytes_accessed=nbytes)


def local(body, name, flops, out_shape, args, scratch=(), grant=16):
    spec = pl.BlockSpec(memory_space=pltpu.VMEM)
    many = isinstance(out_shape, tuple)
    return pl.pallas_call(
        body,
        out_shape=out_shape,
        in_specs=[spec] * len(args),
        out_specs=tuple(spec for _ in out_shape) if many else spec,
        scratch_shapes=list(scratch),
        compiler_params=pltpu.CompilerParams(vmem_limit_bytes=grant << 20),
        cost_estimate=cost(flops, 1000000),
        name=name,
    )(*args)


def dot(a, b):
    return jnp.dot(a, b, preferred_element_type=F32)


def dot_t(a, b):
    return lax.dot_general(a, b, (((0,), (0,)), ((), ())), preferred_element_type=F32)


def write_columns(row, out, at):
    wide = row.astype(F32)
    col = lax.broadcasted_iota(jnp.int32, (512, C), 0) & 63
    out[at, :, 0:C] = jnp.where(col == 0, 0.0, pltpu.roll(wide, 1, 0)).astype(BF)
    out[at, :, C : 2 * C] = row
    out[at, :, 2 * C : 3 * C] = jnp.where(col == 63, 0.0, pltpu.roll(wide, 511, 0)).astype(BF)


def edges_body(x_ref, down_ref, up_ref, sem):
    down = pltpu.make_async_copy(x_ref.at[:, 3], down_ref, sem.at[0])
    up = pltpu.make_async_copy(x_ref.at[:, 0], up_ref, sem.at[1])
    down.start()
    up.start()
    down.wait()
    up.wait()


def edges(x):
    spec = pl.BlockSpec(memory_space=pltpu.VMEM)
    return pl.pallas_call(
        edges_body,
        out_shape=(sds((8, 64, C), BF), sds((8, 64, C), BF)),
        in_specs=[pl.BlockSpec(memory_space=pl.ANY)],
        out_specs=(spec, spec),
        scratch_shapes=[pltpu.SemaphoreType.DMA((2,))],
        compiler_params=pltpu.CompilerParams(vmem_limit_bytes=4 << 20),
        name="edges",
    )(x)


def inner_body(x_ref, sk_ref, st_ref, tk_ref, tt_ref, x6_ref, acc_ref, w_ref, tw_ref, tkt_ref, x_vmem, sem):
    load = pltpu.make_async_copy(x_ref, x_vmem, sem)
    load.start()
    w_ref[:, :, 0:C] = sk_ref[...]
    w_ref[:, :, C:384] = jnp.zeros((3, 3 * C, 64), BF)
    w_ref[:, :, 384 : 384 + C] = st_ref[...]
    w_ref[:, :, 384 + C : 768] = jnp.zeros((3, 3 * C, 64), BF)
    tw_ref[C:384] = jnp.zeros((64, 3 * C), BF)
    tw_ref[384 + C : 768] = jnp.zeros((64, 3 * C), BF)
    for k in range(3):
        tw_ref[0:C, k * C : (k + 1) * C] = tt_ref[k]
        tw_ref[384 : 384 + C, k * C : (k + 1) * C] = tk_ref[k]
        tkt_ref[k * C : (k + 1) * C] = tk_ref[k].T
    load.wait()

    def build(r, carry):
        write_columns(x_vmem[:, r].reshape(512, C), x6_ref, r + 1)
        return carry

    lax.fori_loop(0, 4, build, 0)

    def taps(r, carry):
        acc_ref[r] = dot(x6_ref[r + 1], w_ref[1])

        @pl.when(r > 0)
        def _():
            acc_ref[r] += dot(x6_ref[r], w_ref[0])

        @pl.when(r < 3)
        def _():
            acc_ref[r] += dot(x6_ref[r + 2], w_ref[2])

        return carry

    lax.fori_loop(0, 4, taps, 0)


def inner(x, sk, st, tk, tt):
    spec = pl.BlockSpec(memory_space=pltpu.VMEM)
    return pl.pallas_call(
        inner_body,
        out_shape=(
            sds((6, 512, 3 * C), BF),
            sds((4, 512, 768), F32),
            sds((3, 3 * C, 768), BF),
            sds((768, 3 * C), BF),
            sds((3 * C, C), BF),
        ),
        in_specs=[pl.BlockSpec(memory_space=pl.ANY)] + [spec] * 4,
        out_specs=(spec,) * 5,
        scratch_shapes=[pltpu.VMEM((8, 4, 64, C), BF), pltpu.SemaphoreType.DMA],
        compiler_params=pltpu.CompilerParams(vmem_limit_bytes=16 << 20),
        cost_estimate=cost(6300000000, 1000000),
        name="inner",
    )(x, sk, st, tk, tt)


def frame_rows(value, frame):
    return jnp.concatenate([value[frame * 64 : frame * 64 + 64], value[256 + frame * 64 : 320 + frame * 64]])


def outer_body(old_ref, top_ref, bot_ref, w_ref, acc_ref, tw_ref, x6_ref, slope_ref, ad_ref, pn_ref, pp_ref, work_ref):
    write_columns(top_ref[...].reshape(512, C), x6_ref, 0)
    write_columns(bot_ref[...].reshape(512, C), x6_ref, 5)
    work_ref[0] = dot(x6_ref[0], w_ref[0])
    work_ref[1] = jnp.zeros((512, 768), F32)
    work_ref[2] = jnp.zeros((512, 768), F32)
    work_ref[3] = dot(x6_ref[5], w_ref[2])

    def one(r, carry):
        hidden = acc_ref[r, :, 0:C] + work_ref[r, :, 0:C]
        tangent = acc_ref[r, :, 384 : 384 + C] + work_ref[r, :, 384 : 384 + C]
        sig = jax.nn.sigmoid(hidden)
        slope = sig * (1.0 + hidden * (1.0 - sig))
        slope_ref[r] = slope
        ad_ref[r, :, 0:C] = (hidden * sig).astype(BF)
        ad_ref[r, :, C:384] = jnp.zeros((512, 64), BF)
        ad_ref[r, :, 384 : 384 + C] = (slope * tangent).astype(BF)
        ad_ref[r, :, 384 + C : 768] = jnp.zeros((512, 64), BF)
        last = frame_rows(ad_ref[r], 3)
        first = frame_rows(ad_ref[r], 0)
        pn_ref[r] = dot(last, tw_ref[:, 0:C]).astype(BF)
        pp_ref[r] = dot(first, tw_ref[:, 2 * C : 3 * C]).astype(BF)
        return carry

    lax.fori_loop(0, 4, one, 0)


def outer(x6, top, bot, w, acc, tw):
    spec = pl.BlockSpec(memory_space=pltpu.VMEM)
    return pl.pallas_call(
        outer_body,
        out_shape=(
            sds((6, 512, 3 * C), BF),
            sds((4, 512, C), F32),
            sds((4, 512, 768), BF),
            sds((4, 128, C), BF),
            sds((4, 128, C), BF),
        ),
        in_specs=[spec] * 6,
        out_specs=(spec,) * 5,
        input_output_aliases={0: 0},
        scratch_shapes=[pltpu.VMEM((4, 512, 768), F32)],
        compiler_params=pltpu.CompilerParams(vmem_limit_bytes=16 << 20),
        cost_estimate=cost(1500000000, 1000000),
        name="outer",
    )(x6, top, bot, w, acc, tw)


def own_res_body(ad_ref, tw_ref, res_ref, u_ref):
    def one(r, carry):
        u_ref[...] = dot(ad_ref[r], tw_ref[...])
        for clip in range(2):
            o = 256 * clip
            res_ref[r, o : o + 256] = u_ref[o : o + 256, C : 2 * C]
            res_ref[r, o + 64 : o + 256] += u_ref[o : o + 192, 0:C]
            res_ref[r, o : o + 192] += u_ref[o + 64 : o + 256, 2 * C : 3 * C]
        return carry

    lax.fori_loop(0, 4, one, 0)


def own_res(ad, tw):
    scratch = (pltpu.VMEM((512, 3 * C), F32),)
    return local(own_res_body, "own_res", 3000000000, sds((4, 512, C), F32), (ad, tw), scratch)


def close_body(part_ref, before_ref, after_ref, res_ref, first_ref, last_ref):
    for clip in range(2):
        o, h = 256 * clip, 64 * clip
        first = (part_ref[:, o : o + 64] + before_ref[:, h : h + 64].astype(F32)).astype(BF)
        last = (part_ref[:, o + 192 : o + 256] + after_ref[:, h : h + 64].astype(F32)).astype(BF)
        res_ref[:, o : o + 64] = first
        res_ref[:, o + 64 : o + 192] = part_ref[:, o + 64 : o + 192].astype(BF)
        res_ref[:, o + 192 : o + 256] = last
        first_ref[:, h : h + 64] = first
        last_ref[:, h : h + 64] = last


def close(part, before, after):
    shapes = (sds((4, 512, C), BF), sds((4, 128, C), BF), sds((4, 128, C), BF))
    return local(close_body, "close", 2000000, shapes, (part, before, after))


def own_back_body(res_ref, ad_ref, tkt_ref, back_ref, gt_ref, r3_ref):
    gap = jnp.zeros((64, C), BF)

    def one(r, carry):
        for clip in range(2):
            o = 256 * clip
            r3_ref[r, o : o + 192, 0:C] = res_ref[r, o + 64 : o + 256]
            r3_ref[r, o + 192 : o + 256, 0:C] = gap
            r3_ref[r, o : o + 256, C : 2 * C] = res_ref[r, o : o + 256]
            r3_ref[r, o : o + 64, 2 * C : 3 * C] = gap
            r3_ref[r, o + 64 : o + 256, 2 * C : 3 * C] = res_ref[r, o : o + 192]
        back_ref[r] = dot(r3_ref[r], tkt_ref[...])
        return carry

    lax.fori_loop(0, 4, one, 0)
    gt_ref[...] = dot_t(ad_ref[:, :, 0:C].reshape(2048, C), r3_ref[...].reshape(2048, 3 * C))


def own_back(res, ad, tkt):
    shapes = (sds((4, 512, C), F32), sds((C, 3 * C), F32))
    scratch = (pltpu.VMEM((4, 512, 3 * C), BF),)
    return local(own_back_body, "own_back", 3000000000, shapes, (res, ad, tkt), scratch, 24)


def put_columns(out_ref, start, value):
    done = 0
    while done < value.shape[1]:
        j, lane = (start + done) // 128, (start + done) % 128
        n = min(128 - lane, value.shape[1] - done)
        out_ref[j * C : (j + 1) * C, lane : lane + n] = value[:, done : done + n]
        done += n


def half_grads(which, hbt_ref, x6_ref, gt_ref, out_ref):
    def taps(i):
        return dot(hbt_ref[...], x6_ref[i : i + 4].reshape(2048, 3 * C))

    @pl.when(which == 0)
    def _():
        put_columns(out_ref, 0, taps(0))
        put_columns(out_ref, 3 * C, taps(1))

    @pl.when(which == 1)
    def _():
        put_columns(out_ref, 0, taps(2))
        put_columns(out_ref, 3 * C, gt_ref[...])

    out_ref[15 * C : ROWS // 2] = jnp.zeros((ROWS // 2 - 15 * C, 128), F32)


def send_body(core_ref, before_ref, after_ref, back_ref, slope_ref, ad_ref, tkt_ref, gt_ref, x6_ref, out_ref, hbt_ref, all_ref, hb_ref, halo_ref):
    before = before_ref[...].reshape(512, C)
    after = after_ref[...].reshape(512, C)
    halo_ref[0] = dot(before, tkt_ref[2 * C : 3 * C]).reshape(4, 128, C)
    halo_ref[1] = dot(after, tkt_ref[0:C]).reshape(4, 128, C)
    for clip in range(2):
        o, h = 256 * clip, 64 * clip
        first, last = slice(o, o + 64), slice(o + 192, o + 256)
        mid, edge = slice(o + 64, o + 192), slice(h, h + 64)
        hb_ref[:, first] = (slope_ref[:, first] * (back_ref[:, first] + halo_ref[0, :, edge])).astype(BF)
        hb_ref[:, mid] = (slope_ref[:, mid] * back_ref[:, mid]).astype(BF)
        hb_ref[:, last] = (slope_ref[:, last] * (back_ref[:, last] + halo_ref[1, :, edge])).astype(BF)
    act_last = jnp.concatenate([frame_rows(ad_ref[r], 3)[:, 0:C] for r in range(4)])
    act_first = jnp.concatenate([frame_rows(ad_ref[r], 0)[:, 0:C] for r in range(4)])
    all_ref[:, 0:C] = gt_ref[:, 0:C] + dot_t(act_last, after)
    all_ref[:, C : 2 * C] = gt_ref[:, C : 2 * C]
    all_ref[:, 2 * C : 3 * C] = gt_ref[:, 2 * C : 3 * C] + dot_t(act_first, before)
    hbt_ref[...] = hb_ref[...].reshape(2048, C).T
    half_grads(1 - core_ref[0], hbt_ref, x6_ref, all_ref, out_ref)


def keep_body(core_ref, hbt_ref, x6_ref, gt_ref, out_ref):
    half_grads(core_ref[0], hbt_ref, x6_ref, gt_ref, out_ref)


def grads_send(core, *args):
    spec = pl.BlockSpec(memory_space=pltpu.VMEM)
    return pl.pallas_call(
        send_body,
        out_shape=(sds((ROWS // 2, 128), F32), sds((C, 2048), BF), sds((C, 3 * C), F32)),
        in_specs=[pl.BlockSpec(memory_space=pltpu.SMEM)] + [spec] * len(args),
        out_specs=(spec,) * 3,
        scratch_shapes=[pltpu.VMEM((4, 512, C), BF), pltpu.VMEM((2, 4, 128, C), F32)],
        compiler_params=pltpu.CompilerParams(vmem_limit_bytes=16 << 20),
        cost_estimate=cost(2500000000, 1000000),
        name="grads_send",
    )(core, *args)


def grads_keep(core, *args):
    spec = pl.BlockSpec(memory_space=pltpu.VMEM)
    return pl.pallas_call(
        keep_body,
        out_shape=sds((ROWS // 2, 128), F32),
        in_specs=[pl.BlockSpec(memory_space=pltpu.SMEM)] + [spec] * len(args),
        out_specs=spec,
        compiler_params=pltpu.CompilerParams(vmem_limit_bytes=16 << 20),
        cost_estimate=cost(2500000000, 1000000),
        name="grads_keep",
    )(core, *args)


def block(j):
    at = j * C if j < 15 else ROWS // 2 + (j - 15) * C
    return slice(at, at + C)


def unpack(core, own, other, scale_s, scale_t):
    def body(core_ref, own_ref, other_ref, gs_ref, gt_ref, buf_ref):
        at = core_ref[0]
        half = ROWS // 2
        buf_ref[pl.ds(at * half, half)] = own_ref[...]
        buf_ref[pl.ds((1 - at) * half, half)] = other_ref[...]
        for j in range(22):
            gs_ref[j * 128 : j * 128 + 128] = buf_ref[block(j)].T * scale_s
        gs_ref[22 * 128 : 9 * C] = buf_ref[block(22)].T[0:64] * scale_s
        for k in range(3):
            done = 0
            while done < C:
                j, lane = ((9 + k) * C + done) // 128, ((9 + k) * C + done) % 128
                n = min(128 - lane, C - done)
                gt_ref[k, :, done : done + n] = buf_ref[block(j), lane : lane + n] * scale_t
                done += n

    return pl.pallas_call(
        body,
        out_shape=(sds((9 * C, C), F32), sds((3, C, C), F32)),
        compiler_params=pltpu.CompilerParams(vmem_limit_bytes=32 << 20),
        in_specs=[
            pl.BlockSpec(memory_space=pltpu.SMEM),
            pl.BlockSpec(memory_space=pltpu.VMEM),
            pl.BlockSpec(memory_space=pltpu.VMEM),
        ],
        scratch_shapes=[pltpu.VMEM((ROWS, 128), F32)],
        cost_estimate=cost(2000000, 10000000),
        name="unpack",
    )(core, own, other)


def to_next(value, axis):
    n = lax.axis_size(axis)
    return lax.ppermute(value, axis, [(i, i + 1) for i in range(n - 1)])


def to_prev(value, axis):
    n = lax.axis_size(axis)
    return lax.ppermute(value, axis, [(i + 1, i) for i in range(n - 1)])


def per_device(latents, spatial_kernel, temporal_kernel, spatial_tangent, temporal_tangent):
    x = latents.reshape(8, 4, 64, C)
    core = lax.axis_index("clip").astype(jnp.int32).reshape(1)
    down, up = edges(x)
    top, bot = to_next(down, "band"), to_prev(up, "band")
    x6, acc, w, tw, tkt = inner(
        x,
        spatial_kernel.reshape(3, 3 * C, C),
        spatial_tangent.reshape(3, 3 * C, C),
        temporal_kernel,
        temporal_tangent,
    )
    x6, slope, ad, p_next, p_prev = outer(x6, top, bot, w, acc, tw)
    before, after = to_next(p_next, "frame"), to_prev(p_prev, "frame")
    res, first, last = close(own_res(ad, tw), before, after)
    before, after = to_next(last, "frame"), to_prev(first, "frame")
    back, gt = own_back(res, ad, tkt)
    send, hbt, gt = grads_send(core, before, after, back, slope, ad, tkt, gt, x6)
    keep = grads_keep(core, hbt, x6, gt)
    own, other = reduce_all(send, keep)
    count = 1.0 * latents.shape[0] * latents.shape[1] * latents.shape[2] * latents.shape[3]
    count = count * lax.axis_size("clip") * lax.axis_size("frame") * lax.axis_size("band")
    gs, gt = unpack(core, own, other, (9.0 * C) ** 0.5 / count, (3.0 * C) ** 0.5 / count)
    return gs.reshape(3, 3, C, C), gt


def solution(mesh):
    in_specs = (P("clip", "frame", "band", None, None), P(), P(), P(), P())
    return jax.shard_map(
        per_device, mesh=mesh, in_specs=in_specs, out_specs=(P(), P()), check_vma=False
    )
```

```python
import jax
import jax.numpy as jnp
from jax import lax
from jax.experimental import pallas as pl
from jax.experimental.pallas import tpu as pltpu
from jax.sharding import PartitionSpec as P

BF, F32 = jnp.bfloat16, jnp.float32
C = 320

RING = ("frame", "band")
UNIT = 152
ROWS = 64 * UNIT


def place(y, x, z):
    return (2 * y + x % 2) * 16 + 2 * z + x // 2


def ring_perm(axis, step):
    pairs = []
    for y in range(4):
        for x in range(4):
            for z in range(8):
                if axis == "x":
                    to = place(y, (x + step) % 4, z)
                elif axis == "y":
                    to = place((y + step) % 4, x, z)
                else:
                    to = place(y, x, (z + step) % 8)
                pairs.append((place(y, x, z), to))
    return pairs


def steps_of(count):
    order = []
    for s in range(1, count // 2):
        order += [s, -s]
    return [count // 2] + order[::-1]


def pick(parts, index):
    return lax.dynamic_index_in_dim(parts, index, 0, keepdims=False)


def send_scatter(parts, axis, at):
    count = parts.shape[0]
    return [
        lax.ppermute(pick(parts, (at + s) % count), RING, ring_perm(axis, s))
        for s in steps_of(count)
    ]


def send_gather(mine, axis, count):
    return [lax.ppermute(mine, RING, ring_perm(axis, s)) for s in steps_of(count)]


def arrange(mine, got, at):
    count = len(got) + 1
    whole = jnp.zeros((count,) + mine.shape, mine.dtype)
    whole = lax.dynamic_update_index_in_dim(whole, mine, at, 0)
    for s, piece in zip(steps_of(count), got):
        whole = lax.dynamic_update_index_in_dim(whole, piece, (at - s) % count, 0)
    return whole


def reduce_all(send, keep):
    frame = lax.axis_index("frame")
    band = lax.axis_index("band")
    y = frame // 2
    x = frame % 2 + 2 * (band % 2)
    z = band // 2
    swap = [(0, 1), (1, 0)]
    half = (keep + lax.ppermute(send, "clip", swap)).reshape(2, 4, 4, UNIT, 128)
    a, b = half[0], half[1]
    ga, gb = send_scatter(a, "x", x), send_scatter(b, "y", y)
    a = sum(ga, pick(a, x))
    b = sum(gb, pick(b, y))
    ga, gb = send_scatter(a, "y", y), send_scatter(b, "x", x)
    a = sum(ga, pick(a, y))
    b = sum(gb, pick(b, x))
    both = jnp.concatenate([a, b, jnp.zeros((16, 128), a.dtype)])
    parts = both.reshape(2, 160, 128)
    side = z & 1
    pair = [(place(y, x, z), place(y, x, z ^ 1)) for y in range(4) for x in range(4) for z in range(8)]
    both = pick(parts, side) + lax.ppermute(pick(parts, 1 - side), RING, pair)
    far, near, back = [lax.ppermute(both, RING, ring_perm("z", s)) for s in (4, 2, -2)]
    both = (both + far) + (near + back)
    other = lax.ppermute(both, RING, pair)
    low = side == 0
    both = jnp.concatenate([jnp.where(low, both, other), jnp.where(low, other, both)])
    a, b = both[:UNIT], both[UNIT : 2 * UNIT]
    ga, gb = send_gather(a, "y", 4), send_gather(b, "x", 4)
    a, b = arrange(a, ga, y), arrange(b, gb, x)
    ga, gb = send_gather(a, "x", 4), send_gather(b, "y", 4)
    a, b = arrange(a, ga, x), arrange(b, gb, y)
    half = jnp.stack([a, b])
    other = lax.ppermute(half, "clip", swap)
    return half.reshape(ROWS // 2, 128), other.reshape(ROWS // 2, 128)


def sds(shape, dtype):
    return jax.ShapeDtypeStruct(shape, dtype)


def cost(flops, nbytes):
    return pl.CostEstimate(flops=flops, transcendentals=0, bytes_accessed=nbytes)


def call(body, name, ins, outs, args, scratch=(), grant=16, flops=1000000000, alias=None):
    kinds = {"v": pltpu.VMEM, "h": pltpu.HBM, "s": pltpu.SMEM}
    args = [pltpu.with_memory_space_constraint(a, pltpu.HBM) if k == "h" else a for k, a in zip(ins, args)]
    return pl.pallas_call(
        body,
        out_shape=tuple(pltpu.HBM(a.shape, a.dtype) if k == "h" else a for k, a in outs),
        in_specs=[pl.BlockSpec(memory_space=kinds[k]) for k in ins],
        out_specs=tuple(pl.BlockSpec(memory_space=kinds[k]) for k, _ in outs),
        input_output_aliases=alias or {},
        scratch_shapes=list(scratch),
        compiler_params=pltpu.CompilerParams(vmem_limit_bytes=grant << 20),
        cost_estimate=cost(flops, 1000000),
        name=name,
    )(*args)


def start(src, dst, sem):
    copy = pltpu.make_async_copy(src, dst, sem)
    copy.start()
    return copy


def dot(a, b):
    return jnp.dot(a, b, preferred_element_type=F32)


def dot_t(a, b):
    return lax.dot_general(a, b, (((0,), (0,)), ((), ())), preferred_element_type=F32)


def write_columns(row, out, at):
    wide = row.astype(F32)
    col = lax.broadcasted_iota(jnp.int32, (512, C), 0) & 63
    out[at, :, 0:C] = jnp.where(col == 0, 0.0, pltpu.roll(wide, 1, 0)).astype(BF)
    out[at, :, C : 2 * C] = row
    out[at, :, 2 * C : 3 * C] = jnp.where(col == 63, 0.0, pltpu.roll(wide, 511, 0)).astype(BF)


def edges_body(x_ref, down_ref, up_ref, sem):
    down = start(x_ref.at[:, 3], down_ref, sem.at[0])
    up = start(x_ref.at[:, 0], up_ref, sem.at[1])
    down.wait()
    up.wait()


def edges(x):
    outs = [("v", sds((8, 64, C), BF))] * 2
    return call(edges_body, "edges", "h", outs, (x,), (pltpu.SemaphoreType.DMA((2,)),), 4, 1000)


def frame_rows(value, frame):
    return jnp.concatenate([value[frame * 64 : frame * 64 + 64], value[256 + frame * 64 : 320 + frame * 64]])


def activate(m, hidden, tangent, tw_ref, slope_ref, ad_ref, act_ref, edge_ref, pn_ref, pp_ref):
    sig = jax.nn.sigmoid(hidden)
    slope = sig * (1.0 + hidden * (1.0 - sig))
    slope_ref[m] = slope
    active = (hidden * sig).astype(BF)
    act_ref[m] = active
    ad_ref[m, :, 0:C] = active
    ad_ref[m, :, C:384] = jnp.zeros((512, 64), BF)
    ad_ref[m, :, 384 : 384 + C] = (slope * tangent).astype(BF)
    ad_ref[m, :, 384 + C : 768] = jnp.zeros((512, 64), BF)
    first = frame_rows(ad_ref[m], 0)
    last = frame_rows(ad_ref[m], 3)
    edge_ref[0, m] = first[:, 0:C]
    edge_ref[1, m] = last[:, 0:C]
    pn_ref[m] = dot(last, tw_ref[:, 0:C]).astype(BF)
    pp_ref[m] = dot(first, tw_ref[:, 2 * C : 3 * C]).astype(BF)


GROUP = [
    ("h", jax.ShapeDtypeStruct((2, 512, C), F32)),
    ("v", jax.ShapeDtypeStruct((2, 512, 768), BF)),
    ("h", jax.ShapeDtypeStruct((2, 512, C), BF)),
    ("h", jax.ShapeDtypeStruct((2, 2, 128, C), BF)),
    ("v", jax.ShapeDtypeStruct((2, 128, C), BF)),
    ("v", jax.ShapeDtypeStruct((2, 128, C), BF)),
]
GROUP_VMEM = (
    pltpu.VMEM((2, 512, C), F32),
    pltpu.VMEM((2, 512, C), BF),
    pltpu.VMEM((2, 2, 128, C), BF),
)


def inner_body(
    x_ref, sk_ref, st_ref, tk_ref, tt_ref,
    x6_ref, acc_out, w_out, tw_ref, tkt_ref, slope_ref, ad_ref, act_ref, edge_ref, pn_ref, pp_ref,
    slope_v, act_v, edge_v, acc_ref, w_ref, x_v, sk_v, st_v, tk_v, tt_v, x4, mid, tkt_v, sem,
):
    loads = [
        start(src, dst, sem.at[i])
        for i, (src, dst) in enumerate(
            ((x_ref, x_v), (sk_ref, sk_v), (st_ref, st_v), (tk_ref, tk_v), (tt_ref, tt_v))
        )
    ]
    w_ref[:, :, C:384] = jnp.zeros((2, 3 * C, 64), BF)
    w_ref[:, :, 384 + C : 768] = jnp.zeros((2, 3 * C, 64), BF)
    mid[:, C:384] = jnp.zeros((3 * C, 64), BF)
    mid[:, 384 + C : 768] = jnp.zeros((3 * C, 64), BF)
    tw_ref[C:384] = jnp.zeros((64, 3 * C), BF)
    tw_ref[384 + C : 768] = jnp.zeros((64, 3 * C), BF)
    loads[0].wait()

    def build(r, carry):
        write_columns(x_v[:, r].reshape(512, C), x4, r)
        return carry

    lax.fori_loop(0, 4, build, 0)
    keep = start(x4, x6_ref.at[1:5], sem.at[5])
    loads[1].wait()
    w_ref[0, :, 0:C] = sk_v[0]
    w_ref[1, :, 0:C] = sk_v[2]
    mid[:, 0:C] = sk_v[1]
    loads[2].wait()
    w_ref[0, :, 384 : 384 + C] = st_v[0]
    w_ref[1, :, 384 : 384 + C] = st_v[2]
    mid[:, 384 : 384 + C] = st_v[1]
    sides = start(w_ref, w_out, sem.at[10])
    loads[3].wait()
    loads[4].wait()
    for k in range(3):
        tw_ref[0:C, k * C : (k + 1) * C] = tt_v[k]
        tw_ref[384 : 384 + C, k * C : (k + 1) * C] = tk_v[k]
        tkt_v[k * C : (k + 1) * C] = tk_v[k].T
    turned = start(tkt_v, tkt_ref, sem.at[6])

    def middle(m, carry):
        acc_ref[m] = dot(x4[m], w_ref[0])
        acc_ref[m] += dot(x4[m + 1], mid[...])
        acc_ref[m] += dot(x4[m + 2], w_ref[1])
        activate(
            m, acc_ref[m, :, 0:C], acc_ref[m, :, 384 : 384 + C],
            tw_ref, slope_v, ad_ref, act_v, edge_v, pn_ref, pp_ref,
        )
        return carry

    lax.fori_loop(0, 2, middle, 0)
    saves = [
        start(src, dst, sem.at[7 + i])
        for i, (src, dst) in enumerate(((slope_v, slope_ref), (act_v, act_ref), (edge_v, edge_ref)))
    ]

    def ends(e, carry):
        acc_ref[e] = dot(x4[3 * e], mid[...])
        acc_ref[e] += dot(x4[1 + e], w_ref[1 - e])
        return carry

    lax.fori_loop(0, 2, ends, 0)
    for copy in [keep, turned, sides, start(acc_ref, acc_out, sem.at[11])] + saves:
        copy.wait()


def inner(*args):
    outs = [
        ("h", sds((6, 512, 3 * C), BF)),
        ("h", sds((2, 512, 768), F32)),
        ("h", sds((2, 3 * C, 768), BF)),
        ("v", sds((768, 3 * C), BF)),
        ("h", sds((3 * C, C), BF)),
    ] + GROUP
    scratch = GROUP_VMEM + (
        pltpu.VMEM((2, 512, 768), F32),
        pltpu.VMEM((2, 3 * C, 768), BF),
        pltpu.VMEM((8, 4, 64, C), BF),
        pltpu.VMEM((3, 3 * C, C), BF),
        pltpu.VMEM((3, 3 * C, C), BF),
        pltpu.VMEM((3, C, C), BF),
        pltpu.VMEM((3, C, C), BF),
        pltpu.VMEM((4, 512, 3 * C), BF),
        pltpu.VMEM((3 * C, 768), BF),
        pltpu.VMEM((3 * C, C), BF),
        pltpu.SemaphoreType.DMA((12,)),
    )
    return call(inner_body, "inner", "hhhhh", outs, args, scratch, 32, 6000000000)


def outer_body(
    old_ref, top_ref, bot_ref, w_in, acc_in, tw_ref,
    x6_ref, slope_ref, ad_ref, act_ref, edge_ref, pn_ref, pp_ref,
    slope_v, act_v, edge_v, x2, rows, sum_v, w_ref, acc_ref, sem,
):
    loads = [start(w_in, w_ref, sem.at[5]), start(acc_in, acc_ref, sem.at[6])]
    rows[0] = top_ref[...].reshape(512, C)
    rows[1] = bot_ref[...].reshape(512, C)

    def build(e, carry):
        write_columns(rows[e], x2, e)
        return carry

    lax.fori_loop(0, 2, build, 0)
    saves = [start(x2.at[e], x6_ref.at[5 * e], sem.at[e]) for e in range(2)]
    for copy in loads:
        copy.wait()

    def ends(e, carry):
        sum_v[...] = acc_ref[e] + dot(x2[e], w_ref[e])
        activate(
            e, sum_v[:, 0:C], sum_v[:, 384 : 384 + C],
            tw_ref, slope_v, ad_ref, act_v, edge_v, pn_ref, pp_ref,
        )
        return carry

    lax.fori_loop(0, 2, ends, 0)
    saves += [
        start(src, dst, sem.at[2 + i])
        for i, (src, dst) in enumerate(((slope_v, slope_ref), (act_v, act_ref), (edge_v, edge_ref)))
    ]
    for copy in saves:
        copy.wait()


def outer(*args):
    outs = [("h", sds((6, 512, 3 * C), BF))] + GROUP
    scratch = GROUP_VMEM + (
        pltpu.VMEM((2, 512, 3 * C), BF),
        pltpu.VMEM((2, 512, C), BF),
        pltpu.VMEM((512, 768), F32),
        pltpu.VMEM((2, 3 * C, 768), BF),
        pltpu.VMEM((2, 512, 768), F32),
        pltpu.SemaphoreType.DMA((7,)),
    )
    return call(outer_body, "outer", "hvvhhv", outs, args, scratch, 24, 2000000000, {0: 0})


def own_res_body(ad_ref, tw_ref, part_ref, u_ref):
    def one(r, carry):
        u_ref[...] = dot(ad_ref[r], tw_ref[...])
        for clip in range(2):
            o = 256 * clip
            part_ref[r, o : o + 256] = u_ref[o : o + 256, C : 2 * C]
            part_ref[r, o + 64 : o + 256] += u_ref[o : o + 192, 0:C]
            part_ref[r, o : o + 192] += u_ref[o + 64 : o + 256, 2 * C : 3 * C]
        return carry

    lax.fori_loop(0, 2, one, 0)


def own_res(*args):
    outs = [("v", sds((2, 512, C), F32))]
    return call(own_res_body, "own_res", "vv", outs, args, (pltpu.VMEM((512, 3 * C), F32),))[0]


def close_body(part_ref, before_ref, after_ref, first_ref, last_ref):
    for clip in range(2):
        o, h = 256 * clip, 64 * clip
        edge = slice(h, h + 64)
        first_ref[:, edge] = (part_ref[:, o : o + 64] + before_ref[:, edge].astype(F32)).astype(BF)
        last_ref[:, edge] = (part_ref[:, o + 192 : o + 256] + after_ref[:, edge].astype(F32)).astype(BF)


def close(*args):
    return call(close_body, "close", "vvv", [("v", sds((2, 128, C), BF))] * 2, args, (), 8, 1000000)


def own_back_body(part_ref, first_ref, last_ref, act_ref, tkt_ref, back_ref, gt_ref, r3_ref, act_v, tkt_v, sem):
    turned = start(tkt_ref, tkt_v, sem.at[0])
    active = start(act_ref, act_v, sem.at[1])
    gap = jnp.zeros((64, C), BF)

    def build(r, carry):
        for clip in range(2):
            o, h = 256 * clip, 64 * clip
            value = jnp.concatenate(
                [first_ref[r, h : h + 64], part_ref[r, o + 64 : o + 192].astype(BF), last_ref[r, h : h + 64]]
            )
            r3_ref[r, o : o + 192, 0:C] = value[64:256]
            r3_ref[r, o + 192 : o + 256, 0:C] = gap
            r3_ref[r, o : o + 256, C : 2 * C] = value
            r3_ref[r, o : o + 64, 2 * C : 3 * C] = gap
            r3_ref[r, o + 64 : o + 256, 2 * C : 3 * C] = value[0:192]
        return carry

    lax.fori_loop(0, 2, build, 0)
    turned.wait()

    def back(r, carry):
        back_ref[r] = dot(r3_ref[r], tkt_v[...])
        return carry

    lax.fori_loop(0, 2, back, 0)
    active.wait()
    gt_ref[...] = dot_t(act_v[...].reshape(1024, C), r3_ref[...].reshape(1024, 3 * C))


def own_back(*args):
    outs = [("v", sds((2, 512, C), F32)), ("v", sds((C, 3 * C), F32))]
    scratch = (
        pltpu.VMEM((2, 512, 3 * C), BF),
        pltpu.VMEM((2, 512, C), BF),
        pltpu.VMEM((3 * C, C), BF),
        pltpu.SemaphoreType.DMA((2,)),
    )
    return call(own_back_body, "own_back", "vvvhh", outs, args, scratch)


def put_columns(out_ref, start, value):
    done = 0
    while done < value.shape[1]:
        j, lane = (start + done) // 128, (start + done) % 128
        n = min(128 - lane, value.shape[1] - done)
        out_ref[j * C : (j + 1) * C, lane : lane + n] = value[:, done : done + n]
        done += n


def half_grads(which, hbt_ref, x6_v, gt_v, out_ref, turn):
    def one(n, carry):
        tap = 2 * which + n

        @pl.when(tap < 3)
        def _():
            turn[...] = dot(hbt_ref[...], x6_v[pl.ds(tap, 4)].reshape(2048, 3 * C))

        @pl.when(tap == 3)
        def _():
            turn[...] = gt_v[...]

        @pl.when(n == 0)
        def _():
            put_columns(out_ref, 0, turn[...])

        @pl.when(n == 1)
        def _():
            put_columns(out_ref, 3 * C, turn[...])

        return carry

    lax.fori_loop(0, 2, one, 0)
    out_ref[15 * C : ROWS // 2] = jnp.zeros((ROWS // 2 - 15 * C, 128), F32)


def send_body(
    core_ref, bm_ref, am_ref, be_ref, ae_ref, backm_ref, backe_ref, gtm_ref, gte_ref,
    slopem_ref, slopee_ref, edgem_ref, edgee_ref, tkt_ref, x6_ref,
    out_ref, hbt_ref, gt_ref,
    slope_v, edge_v, tkt_v, x6_v, hb, halo, gt_v, turn, sem,
):
    loads = [
        start(src, dst, sem.at[i])
        for i, (src, dst) in enumerate(
            (
                (tkt_ref, tkt_v),
                (slopem_ref, slope_v.at[0]),
                (slopee_ref, slope_v.at[1]),
                (edgem_ref, edge_v.at[0]),
                (edgee_ref, edge_v.at[1]),
                (x6_ref, x6_v),
            )
        )
    ]
    loads[0].wait()
    for g, (before, after) in enumerate(((bm_ref, am_ref), (be_ref, ae_ref))):
        halo[g, 0] = dot(before[...].reshape(256, C), tkt_v[2 * C : 3 * C]).reshape(2, 128, C)
        halo[g, 1] = dot(after[...].reshape(256, C), tkt_v[0:C]).reshape(2, 128, C)
    for g, (back_ref, rows) in enumerate(((backm_ref, (1, 2)), (backe_ref, (0, 3)))):
        loads[1 + g].wait()
        for m, r in enumerate(rows):
            for clip in range(2):
                o, h = 256 * clip, 64 * clip
                first, last = slice(o, o + 64), slice(o + 192, o + 256)
                mid, edge = slice(o + 64, o + 192), slice(h, h + 64)
                hb[r, first] = (slope_v[g, m, first] * (back_ref[m, first] + halo[g, 0, m, edge])).astype(BF)
                hb[r, mid] = (slope_v[g, m, mid] * back_ref[m, mid]).astype(BF)
                hb[r, last] = (slope_v[g, m, last] * (back_ref[m, last] + halo[g, 1, m, edge])).astype(BF)
    loads[3].wait()
    loads[4].wait()
    before = jnp.concatenate([bm_ref[...].reshape(256, C), be_ref[...].reshape(256, C)])
    after = jnp.concatenate([am_ref[...].reshape(256, C), ae_ref[...].reshape(256, C)])
    gt_v[:, 0:C] = gtm_ref[:, 0:C] + gte_ref[:, 0:C] + dot_t(edge_v[:, 1].reshape(512, C), after)
    gt_v[:, C : 2 * C] = gtm_ref[:, C : 2 * C] + gte_ref[:, C : 2 * C]
    gt_v[:, 2 * C : 3 * C] = (
        gtm_ref[:, 2 * C : 3 * C] + gte_ref[:, 2 * C : 3 * C] + dot_t(edge_v[:, 0].reshape(512, C), before)
    )
    save = start(gt_v, gt_ref, sem.at[6])
    hbt_ref[...] = hb[...].reshape(2048, C).T
    loads[5].wait()
    half_grads(1 - core_ref[0], hbt_ref, x6_v, gt_v, out_ref, turn)
    save.wait()


def grads_send(*args):
    outs = [("v", sds((ROWS // 2, 128), F32)), ("v", sds((C, 2048), BF)), ("h", sds((C, 3 * C), F32))]
    scratch = (
        pltpu.VMEM((2, 2, 512, C), F32),
        pltpu.VMEM((2, 2, 2, 128, C), BF),
        pltpu.VMEM((3 * C, C), BF),
        pltpu.VMEM((6, 512, 3 * C), BF),
        pltpu.VMEM((4, 512, C), BF),
        pltpu.VMEM((2, 2, 2, 128, C), F32),
        pltpu.VMEM((C, 3 * C), F32),
        pltpu.VMEM((C, 3 * C), F32),
        pltpu.SemaphoreType.DMA((7,)),
    )
    return call(send_body, "grads_send", "svvvvvvvvhhhhhh", outs, args, scratch, 24, 2500000000)


def keep_body(core_ref, hbt_ref, x6_ref, gt_ref, out_ref, x6_v, gt_v, turn, sem):
    loads = [start(x6_ref, x6_v, sem.at[0]), start(gt_ref, gt_v, sem.at[1])]
    for copy in loads:
        copy.wait()
    half_grads(core_ref[0], hbt_ref, x6_v, gt_v, out_ref, turn)


def grads_keep(*args):
    scratch = (
        pltpu.VMEM((6, 512, 3 * C), BF),
        pltpu.VMEM((C, 3 * C), F32),
        pltpu.VMEM((C, 3 * C), F32),
        pltpu.SemaphoreType.DMA((2,)),
    )
    outs = [("v", sds((ROWS // 2, 128), F32))]
    return call(keep_body, "grads_keep", "svhh", outs, args, scratch, 24, 2500000000)[0]


def block(j):
    at = j * C if j < 15 else ROWS // 2 + (j - 15) * C
    return slice(at, at + C)


def unpack(core, own, other, scale_s, scale_t):
    def body(core_ref, own_ref, other_ref, gs_ref, gt_ref, buf_ref):
        at = core_ref[0]
        half = ROWS // 2
        buf_ref[pl.ds(at * half, half)] = own_ref[...]
        buf_ref[pl.ds((1 - at) * half, half)] = other_ref[...]

        def one(j, carry):
            at = pl.multiple_of(j * C + jnp.where(j < 15, 0, ROWS // 2 - 15 * C), 8)
            gs_ref[pl.ds(pl.multiple_of(j * 128, 128), 128)] = buf_ref[pl.ds(at, C)].T * scale_s
            return carry

        lax.fori_loop(0, 22, one, 0)
        gs_ref[22 * 128 : 9 * C] = buf_ref[block(22)].T[0:64] * scale_s
        for k in range(3):
            done = 0
            while done < C:
                j, lane = ((9 + k) * C + done) // 128, ((9 + k) * C + done) % 128
                n = min(128 - lane, C - done)
                gt_ref[k, :, done : done + n] = buf_ref[block(j), lane : lane + n] * scale_t
                done += n

    return pl.pallas_call(
        body,
        out_shape=(sds((9 * C, C), F32), sds((3, C, C), F32)),
        compiler_params=pltpu.CompilerParams(vmem_limit_bytes=32 << 20),
        in_specs=[
            pl.BlockSpec(memory_space=pltpu.SMEM),
            pl.BlockSpec(memory_space=pltpu.VMEM),
            pl.BlockSpec(memory_space=pltpu.VMEM),
        ],
        scratch_shapes=[pltpu.VMEM((ROWS, 128), F32)],
        cost_estimate=cost(2000000, 10000000),
        name="unpack",
    )(core, own, other)


def to_next(value, axis):
    n = lax.axis_size(axis)
    return lax.ppermute(value, axis, [(i, i + 1) for i in range(n - 1)])


def to_prev(value, axis):
    n = lax.axis_size(axis)
    return lax.ppermute(value, axis, [(i + 1, i) for i in range(n - 1)])


def per_device(latents, spatial_kernel, temporal_kernel, spatial_tangent, temporal_tangent):
    x = latents.reshape(8, 4, 64, C)
    core = lax.axis_index("clip").astype(jnp.int32).reshape(1)
    down, up = edges(x)
    top, bot = to_next(down, "band"), to_prev(up, "band")
    x6, acc, w, tw, tkt, slope_m, ad_m, act_m, edge_m, pn_m, pp_m = inner(
        x,
        spatial_kernel.reshape(3, 3 * C, C),
        spatial_tangent.reshape(3, 3 * C, C),
        temporal_kernel,
        temporal_tangent,
    )
    pn_m, pp_m = to_next(pn_m, "frame"), to_prev(pp_m, "frame")
    x6, slope_e, ad_e, act_e, edge_e, pn_e, pp_e = outer(x6, top, bot, w, acc, tw)
    pn_e, pp_e = to_next(pn_e, "frame"), to_prev(pp_e, "frame")
    part_m = own_res(ad_m, tw)
    first_m, last_m = close(part_m, pn_m, pp_m)
    before_m, after_m = to_next(last_m, "frame"), to_prev(first_m, "frame")
    part_e = own_res(ad_e, tw)
    first_e, last_e = close(part_e, pn_e, pp_e)
    before_e, after_e = to_next(last_e, "frame"), to_prev(first_e, "frame")
    back_m, gt_m = own_back(part_m, first_m, last_m, act_m, tkt)
    back_e, gt_e = own_back(part_e, first_e, last_e, act_e, tkt)
    send, hbt, gt = grads_send(
        core, before_m, after_m, before_e, after_e, back_m, back_e, gt_m, gt_e,
        slope_m, slope_e, edge_m, edge_e, tkt, x6,
    )
    keep = grads_keep(core, hbt, x6, gt)
    own, other = reduce_all(send, keep)
    count = 1.0 * latents.shape[0] * latents.shape[1] * latents.shape[2] * latents.shape[3]
    count = count * lax.axis_size("clip") * lax.axis_size("frame") * lax.axis_size("band")
    gs, gt = unpack(core, own, other, (9.0 * C) ** 0.5 / count, (3.0 * C) ** 0.5 / count)
    return gs.reshape(3, 3, C, C), gt


def solution(mesh):
    in_specs = (P("clip", "frame", "band", None, None), P(), P(), P(), P())
    return jax.shard_map(
        per_device, mesh=mesh, in_specs=in_specs, out_specs=(P(), P()), check_vma=False
    )
```

```python
import jax
import jax.numpy as jnp
from jax import lax
from jax.experimental import pallas as pl
from jax.experimental.pallas import tpu as pltpu
from jax.sharding import PartitionSpec as P

BF, F32 = jnp.bfloat16, jnp.float32
C = 320

RING = ("frame", "band")
UNIT = 152
ROWS = 64 * UNIT


def place(y, x, z):
    return (2 * y + x % 2) * 16 + 2 * z + x // 2


def ring_perm(axis, step):
    pairs = []
    for y in range(4):
        for x in range(4):
            for z in range(8):
                if axis == "x":
                    to = place(y, (x + step) % 4, z)
                elif axis == "y":
                    to = place((y + step) % 4, x, z)
                else:
                    to = place(y, x, (z + step) % 8)
                pairs.append((place(y, x, z), to))
    return pairs


def steps_of(count):
    order = []
    for s in range(1, count // 2):
        order += [s, -s]
    return [count // 2] + order[::-1]


def pick(parts, index):
    return lax.dynamic_index_in_dim(parts, index, 0, keepdims=False)


def send_scatter(parts, axis, at):
    count = parts.shape[0]
    return [
        lax.ppermute(pick(parts, (at + s) % count), RING, ring_perm(axis, s))
        for s in steps_of(count)
    ]


def send_gather(mine, axis, count):
    return [lax.ppermute(mine, RING, ring_perm(axis, s)) for s in steps_of(count)]


def arrange(mine, got, at):
    count = len(got) + 1
    whole = jnp.zeros((count,) + mine.shape, mine.dtype)
    whole = lax.dynamic_update_index_in_dim(whole, mine, at, 0)
    for s, piece in zip(steps_of(count), got):
        whole = lax.dynamic_update_index_in_dim(whole, piece, (at - s) % count, 0)
    return whole


def reduce_all(send, keep, ids):
    frame, band = ids[1], ids[2]
    y = frame // 2
    x = frame % 2 + 2 * (band % 2)
    z = band // 2
    swap = [(0, 1), (1, 0)]
    half = (keep + lax.ppermute(send, "clip", swap)).reshape(2, 4, 4, UNIT, 128)
    a, b = half[0], half[1]
    ga, gb = send_scatter(a, "x", x), send_scatter(b, "y", y)
    a = sum(ga, pick(a, x))
    b = sum(gb, pick(b, y))
    ga, gb = send_scatter(a, "y", y), send_scatter(b, "x", x)
    a = sum(ga, pick(a, y))
    b = sum(gb, pick(b, x))
    both = jnp.concatenate([a, b, jnp.zeros((16, 128), a.dtype)])
    parts = both.reshape(2, 160, 128)
    side = z & 1
    pair = [(place(y, x, z), place(y, x, z ^ 1)) for y in range(4) for x in range(4) for z in range(8)]
    both = pick(parts, side) + lax.ppermute(pick(parts, 1 - side), RING, pair)
    far, near, back = [lax.ppermute(both, RING, ring_perm("z", s)) for s in (4, 2, -2)]
    both = (both + far) + (near + back)
    other = lax.ppermute(both, RING, pair)
    low = side == 0
    both = jnp.concatenate([jnp.where(low, both, other), jnp.where(low, other, both)])
    a, b = both[:UNIT], both[UNIT : 2 * UNIT]
    ga, gb = send_gather(a, "y", 4), send_gather(b, "x", 4)
    a, b = arrange(a, ga, y), arrange(b, gb, x)
    ga, gb = send_gather(a, "x", 4), send_gather(b, "y", 4)
    a, b = arrange(a, ga, x), arrange(b, gb, y)
    half = jnp.stack([a, b])
    other = lax.ppermute(half, "clip", swap)
    return half.reshape(ROWS // 2, 128), other.reshape(ROWS // 2, 128)


def sds(shape, dtype):
    return jax.ShapeDtypeStruct(shape, dtype)


def cost(flops, nbytes):
    return pl.CostEstimate(flops=flops, transcendentals=0, bytes_accessed=nbytes)


def call(body, name, ins, outs, args, scratch=(), grant=16, flops=1000000000, through=(), alias=None):
    kinds = {"v": pltpu.VMEM, "h": pltpu.HBM, "s": pltpu.SMEM}
    args = [pltpu.with_memory_space_constraint(a, pltpu.HBM) if k == "h" else a for k, a in zip(ins, args)]
    alias = dict(alias or {})
    count = len(outs)
    outs = list(outs)
    for i in through:
        alias[i] = len(outs)
        outs.append((ins[i], sds(args[i].shape, args[i].dtype)))

    def inner_call(*refs):
        n = len(ins)
        body(*refs[: n + count], *refs[n + len(outs) :])

    return pl.pallas_call(
        inner_call,
        out_shape=tuple(pltpu.HBM(a.shape, a.dtype) if k == "h" else a for k, a in outs),
        in_specs=[pl.BlockSpec(memory_space=kinds[k]) for k in ins],
        out_specs=tuple(pl.BlockSpec(memory_space=kinds[k]) for k, _ in outs),
        input_output_aliases=alias,
        scratch_shapes=list(scratch),
        compiler_params=pltpu.CompilerParams(vmem_limit_bytes=grant << 20),
        cost_estimate=cost(flops, 1000000),
        name=name,
    )(*args)


def start(src, dst, sem):
    copy = pltpu.make_async_copy(src, dst, sem)
    copy.start()
    return copy


def dot(a, b):
    return jnp.dot(a, b, preferred_element_type=F32)


def dot_t(a, b):
    return lax.dot_general(a, b, (((0,), (0,)), ((), ())), preferred_element_type=F32)


def write_columns(row, out, at):
    wide = row.astype(F32)
    col = lax.broadcasted_iota(jnp.int32, (512, C), 0) & 63
    out[at, :, 0:C] = jnp.where(col == 0, 0.0, pltpu.roll(wide, 1, 0)).astype(BF)
    out[at, :, C : 2 * C] = row
    out[at, :, 2 * C : 3 * C] = jnp.where(col == 63, 0.0, pltpu.roll(wide, 511, 0)).astype(BF)


def edges_body(x_ref, ids_ref, down_ref, up_ref, same_ref, sem):
    for i in range(3):
        same_ref[i] = ids_ref[i]
    down = start(x_ref.at[:, 3], down_ref, sem.at[0])
    up = start(x_ref.at[:, 0], up_ref, sem.at[1])
    down.wait()
    up.wait()


def edges(x, ids):
    outs = [("v", sds((8, 64, C), BF))] * 2 + [("s", sds((3,), jnp.int32))]
    return call(edges_body, "edges", "hs", outs, (x, ids), (pltpu.SemaphoreType.DMA((2,)),), 4, 1000)


def inner_body(
    x_ref, sk_ref, st_ref, tk_ref, tt_ref,
    x6_ref, acc_ref, w_ref, tw_ref, tkt_ref,
    x_v, sk_v, st_v, tk_v, tt_v, sem,
):
    loads = [
        start(src, dst, sem.at[i])
        for i, (src, dst) in enumerate(
            ((x_ref, x_v), (sk_ref, sk_v), (st_ref, st_v), (tk_ref, tk_v), (tt_ref, tt_v))
        )
    ]
    w_ref[:, :, C:384] = jnp.zeros((3, 3 * C, 64), BF)
    w_ref[:, :, 384 + C : 768] = jnp.zeros((3, 3 * C, 64), BF)
    tw_ref[C:384] = jnp.zeros((64, 3 * C), BF)
    tw_ref[384 + C : 768] = jnp.zeros((64, 3 * C), BF)
    loads[0].wait()

    def build(r, carry):
        write_columns(x_v[:, r].reshape(512, C), x6_ref, r + 1)
        return carry

    lax.fori_loop(0, 4, build, 0)
    loads[1].wait()
    w_ref[:, :, 0:C] = sk_v[...]
    loads[2].wait()
    w_ref[:, :, 384 : 384 + C] = st_v[...]
    loads[3].wait()
    loads[4].wait()
    for k in range(3):
        tw_ref[0:C, k * C : (k + 1) * C] = tt_v[k]
        tw_ref[384 : 384 + C, k * C : (k + 1) * C] = tk_v[k]
        tkt_ref[k * C : (k + 1) * C] = tk_v[k].T

    def taps(r, carry):
        acc_ref[r] = dot(x6_ref[r + 1], w_ref[1])

        @pl.when(r > 0)
        def _():
            acc_ref[r] += dot(x6_ref[r], w_ref[0])

        @pl.when(r < 3)
        def _():
            acc_ref[r] += dot(x6_ref[r + 2], w_ref[2])

        return carry

    lax.fori_loop(0, 4, taps, 0)


def inner(*args):
    outs = [
        ("v", sds((6, 512, 3 * C), BF)),
        ("v", sds((4, 512, 768), F32)),
        ("v", sds((3, 3 * C, 768), BF)),
        ("v", sds((768, 3 * C), BF)),
        ("v", sds((3 * C, C), BF)),
    ]
    scratch = (
        pltpu.VMEM((8, 4, 64, C), BF),
        pltpu.VMEM((3, 3 * C, C), BF),
        pltpu.VMEM((3, 3 * C, C), BF),
        pltpu.VMEM((3, C, C), BF),
        pltpu.VMEM((3, C, C), BF),
        pltpu.SemaphoreType.DMA((5,)),
    )
    return call(inner_body, "inner", "hhhhh", outs, args, scratch, 16, 6000000000)


def frame_rows(value, frame):
    return jnp.concatenate([value[frame * 64 : frame * 64 + 64], value[256 + frame * 64 : 320 + frame * 64]])


def outer_body(old_ref, top_ref, bot_ref, w_ref, acc_ref, tw_ref, tkt_ref, x6_ref, slope_ref, ad_ref, pn_ref, pp_ref, work_ref):
    write_columns(top_ref[...].reshape(512, C), x6_ref, 0)
    write_columns(bot_ref[...].reshape(512, C), x6_ref, 5)
    work_ref[0] = dot(x6_ref[0], w_ref[0])
    work_ref[1] = jnp.zeros((512, 768), F32)
    work_ref[2] = jnp.zeros((512, 768), F32)
    work_ref[3] = dot(x6_ref[5], w_ref[2])

    def one(r, carry):
        hidden = acc_ref[r, :, 0:C] + work_ref[r, :, 0:C]
        tangent = acc_ref[r, :, 384 : 384 + C] + work_ref[r, :, 384 : 384 + C]
        sig = jax.nn.sigmoid(hidden)
        slope = sig * (1.0 + hidden * (1.0 - sig))
        slope_ref[r] = slope
        ad_ref[r, :, 0:C] = (hidden * sig).astype(BF)
        ad_ref[r, :, C:384] = jnp.zeros((512, 64), BF)
        ad_ref[r, :, 384 : 384 + C] = (slope * tangent).astype(BF)
        ad_ref[r, :, 384 + C : 768] = jnp.zeros((512, 64), BF)
        last = frame_rows(ad_ref[r], 3)
        first = frame_rows(ad_ref[r], 0)
        pn_ref[r] = dot(last, tw_ref[:, 0:C]).astype(BF)
        pp_ref[r] = dot(first, tw_ref[:, 2 * C : 3 * C]).astype(BF)
        return carry

    lax.fori_loop(0, 4, one, 0)


def outer(*args):
    outs = [
        ("v", sds((6, 512, 3 * C), BF)),
        ("v", sds((4, 512, C), F32)),
        ("v", sds((4, 512, 768), BF)),
        ("v", sds((4, 128, C), BF)),
        ("v", sds((4, 128, C), BF)),
    ]
    scratch = (pltpu.VMEM((4, 512, 768), F32),)
    return call(outer_body, "outer", "vvvvvvv", outs, args, scratch, 16, 1500000000, (5, 6), {0: 0})


def own_res_body(ad_ref, tw_ref, x6_ref, slope_ref, tkt_ref, res_ref, u_ref):
    def one(r, carry):
        u_ref[...] = dot(ad_ref[r], tw_ref[...])
        for clip in range(2):
            o = 256 * clip
            res_ref[r, o : o + 256] = u_ref[o : o + 256, C : 2 * C]
            res_ref[r, o + 64 : o + 256] += u_ref[o : o + 192, 0:C]
            res_ref[r, o : o + 192] += u_ref[o + 64 : o + 256, 2 * C : 3 * C]
        return carry

    lax.fori_loop(0, 4, one, 0)


def own_res(*args):
    outs = [("v", sds((4, 512, C), F32))]
    scratch = (pltpu.VMEM((512, 3 * C), F32),)
    return call(own_res_body, "own_res", "vvvvv", outs, args, scratch, through=(0, 2, 3, 4))


def close_body(part_ref, before_ref, after_ref, ad_ref, x6_ref, slope_ref, tkt_ref, first_ref, last_ref):
    for clip in range(2):
        o, h = 256 * clip, 64 * clip
        edge = slice(h, h + 64)
        first_ref[:, edge] = (part_ref[:, o : o + 64] + before_ref[:, edge].astype(F32)).astype(BF)
        last_ref[:, edge] = (part_ref[:, o + 192 : o + 256] + after_ref[:, edge].astype(F32)).astype(BF)


def close(*args):
    outs = [("v", sds((4, 128, C), BF))] * 2
    return call(close_body, "close", "vvvvvvv", outs, args, (), 8, 1000000, (0, 3, 4, 5, 6))


def own_back_body(part_ref, first_ref, last_ref, ad_ref, x6_ref, slope_ref, tkt_ref, back_ref, gt_ref, r3_ref):
    gap = jnp.zeros((64, C), BF)

    def one(r, carry):
        for clip in range(2):
            o, h = 256 * clip, 64 * clip
            value = jnp.concatenate(
                [first_ref[r, h : h + 64], part_ref[r, o + 64 : o + 192].astype(BF), last_ref[r, h : h + 64]]
            )
            r3_ref[r, o : o + 192, 0:C] = value[64:256]
            r3_ref[r, o + 192 : o + 256, 0:C] = gap
            r3_ref[r, o : o + 256, C : 2 * C] = value
            r3_ref[r, o : o + 64, 2 * C : 3 * C] = gap
            r3_ref[r, o + 64 : o + 256, 2 * C : 3 * C] = value[0:192]
        back_ref[r] = dot(r3_ref[r], tkt_ref[...])
        return carry

    lax.fori_loop(0, 4, one, 0)
    gt_ref[...] = dot_t(ad_ref[:, :, 0:C].reshape(2048, C), r3_ref[...].reshape(2048, 3 * C))


def own_back(*args):
    outs = [("v", sds((4, 512, C), F32)), ("v", sds((C, 3 * C), F32))]
    scratch = (pltpu.VMEM((4, 512, 3 * C), BF),)
    return call(own_back_body, "own_back", "vvvvvvv", outs, args, scratch, through=(3, 4, 5, 6))


def put_columns(out_ref, start, value):
    done = 0
    while done < value.shape[1]:
        j, lane = (start + done) // 128, (start + done) % 128
        n = min(128 - lane, value.shape[1] - done)
        out_ref[j * C : (j + 1) * C, lane : lane + n] = value[:, done : done + n]
        done += n


def half_grads(which, hbt_ref, x6_ref, gt_ref, out_ref, turn):
    def one(n, carry):
        tap = 2 * which + n

        @pl.when(tap < 3)
        def _():
            turn[...] = dot(hbt_ref[...], x6_ref[pl.ds(tap, 4)].reshape(2048, 3 * C))

        @pl.when(tap == 3)
        def _():
            turn[...] = gt_ref[...]

        @pl.when(n == 0)
        def _():
            put_columns(out_ref, 0, turn[...])

        @pl.when(n == 1)
        def _():
            put_columns(out_ref, 3 * C, turn[...])

        return carry

    lax.fori_loop(0, 2, one, 0)
    out_ref[15 * C : ROWS // 2] = jnp.zeros((ROWS // 2 - 15 * C, 128), F32)


def send_body(core_ref, before_ref, after_ref, back_ref, slope_ref, ad_ref, tkt_ref, gt_ref, x6_ref, out_ref, hbt_ref, all_ref, hb_ref, halo_ref, turn):
    before = before_ref[...].reshape(512, C)
    after = after_ref[...].reshape(512, C)
    halo_ref[0] = dot(before, tkt_ref[2 * C : 3 * C]).reshape(4, 128, C)
    halo_ref[1] = dot(after, tkt_ref[0:C]).reshape(4, 128, C)
    for clip in range(2):
        o, h = 256 * clip, 64 * clip
        first, last = slice(o, o + 64), slice(o + 192, o + 256)
        mid, edge = slice(o + 64, o + 192), slice(h, h + 64)
        hb_ref[:, first] = (slope_ref[:, first] * (back_ref[:, first] + halo_ref[0, :, edge])).astype(BF)
        hb_ref[:, mid] = (slope_ref[:, mid] * back_ref[:, mid]).astype(BF)
        hb_ref[:, last] = (slope_ref[:, last] * (back_ref[:, last] + halo_ref[1, :, edge])).astype(BF)
    act_last = jnp.concatenate([frame_rows(ad_ref[r], 3)[:, 0:C] for r in range(4)])
    act_first = jnp.concatenate([frame_rows(ad_ref[r], 0)[:, 0:C] for r in range(4)])
    all_ref[:, 0:C] = gt_ref[:, 0:C] + dot_t(act_last, after)
    all_ref[:, C : 2 * C] = gt_ref[:, C : 2 * C]
    all_ref[:, 2 * C : 3 * C] = gt_ref[:, 2 * C : 3 * C] + dot_t(act_first, before)
    hbt_ref[...] = hb_ref[...].reshape(2048, C).T
    half_grads(1 - core_ref[0], hbt_ref, x6_ref, all_ref, out_ref, turn)


def grads_send(*args):
    outs = [("v", sds((ROWS // 2, 128), F32)), ("v", sds((C, 2048), BF)), ("v", sds((C, 3 * C), F32))]
    scratch = (
        pltpu.VMEM((4, 512, C), BF),
        pltpu.VMEM((2, 4, 128, C), F32),
        pltpu.VMEM((C, 3 * C), F32),
    )
    return call(send_body, "grads_send", "svvvvvvvv", outs, args, scratch, 16, 2500000000, (8,))


def keep_body(core_ref, hbt_ref, x6_ref, gt_ref, out_ref, same_ref, turn):
    for i in range(3):
        same_ref[i] = core_ref[i]
    half_grads(core_ref[0], hbt_ref, x6_ref, gt_ref, out_ref, turn)


def grads_keep(*args):
    outs = [("v", sds((ROWS // 2, 128), F32)), ("s", sds((3,), jnp.int32))]
    return call(keep_body, "grads_keep", "svvv", outs, args, (pltpu.VMEM((C, 3 * C), F32),), 16, 2500000000)


def block(j):
    at = j * C if j < 15 else ROWS // 2 + (j - 15) * C
    return slice(at, at + C)


def unpack(core, own, other, scale_s, scale_t):
    def body(core_ref, own_ref, other_ref, gs_ref, gt_ref, buf_ref):
        at = core_ref[0]
        half = ROWS // 2
        buf_ref[pl.ds(at * half, half)] = own_ref[...]
        buf_ref[pl.ds((1 - at) * half, half)] = other_ref[...]
        for j in range(22):
            gs_ref[j * 128 : j * 128 + 128] = buf_ref[block(j)].T * scale_s
        gs_ref[22 * 128 : 9 * C] = buf_ref[block(22)].T[0:64] * scale_s
        for k in range(3):
            done = 0
            while done < C:
                j, lane = ((9 + k) * C + done) // 128, ((9 + k) * C + done) % 128
                n = min(128 - lane, C - done)
                gt_ref[k, :, done : done + n] = buf_ref[block(j), lane : lane + n] * scale_t
                done += n

    return pl.pallas_call(
        body,
        out_shape=(sds((9 * C, C), F32), sds((3, C, C), F32)),
        compiler_params=pltpu.CompilerParams(vmem_limit_bytes=32 << 20),
        in_specs=[
            pl.BlockSpec(memory_space=pltpu.SMEM),
            pl.BlockSpec(memory_space=pltpu.VMEM),
            pl.BlockSpec(memory_space=pltpu.VMEM),
        ],
        scratch_shapes=[pltpu.VMEM((ROWS, 128), F32)],
        cost_estimate=cost(2000000, 10000000),
        name="unpack",
    )(core, own, other)


def to_next(value, axis):
    n = lax.axis_size(axis)
    return lax.ppermute(value, axis, [(i, i + 1) for i in range(n - 1)])


def to_prev(value, axis):
    n = lax.axis_size(axis)
    return lax.ppermute(value, axis, [(i + 1, i) for i in range(n - 1)])


def per_device(latents, spatial_kernel, temporal_kernel, spatial_tangent, temporal_tangent):
    x = latents.reshape(8, 4, 64, C)
    ids = jnp.stack([lax.axis_index(name).astype(jnp.int32) for name in ("clip", "frame", "band")])
    down, up, core = edges(x, ids)
    top, bot = to_next(down, "band"), to_prev(up, "band")
    x6, acc, w, tw, tkt = inner(
        x,
        spatial_kernel.reshape(3, 3 * C, C),
        spatial_tangent.reshape(3, 3 * C, C),
        temporal_kernel,
        temporal_tangent,
    )
    x6, slope, ad, p_next, p_prev, tw, tkt = outer(x6, top, bot, w, acc, tw, tkt)
    before, after = to_next(p_next, "frame"), to_prev(p_prev, "frame")
    part, ad, x6, slope, tkt = own_res(ad, tw, x6, slope, tkt)
    first, last, part, ad, x6, slope, tkt = close(part, before, after, ad, x6, slope, tkt)
    before, after = to_next(last, "frame"), to_prev(first, "frame")
    back, gt, ad, x6, slope, tkt = own_back(part, first, last, ad, x6, slope, tkt)
    send, hbt, gt, x6 = grads_send(core, before, after, back, slope, ad, tkt, gt, x6)
    keep, ids = grads_keep(core, hbt, x6, gt)
    own, other = reduce_all(send, keep, ids)
    count = 1.0 * latents.shape[0] * latents.shape[1] * latents.shape[2] * latents.shape[3]
    count = count * lax.axis_size("clip") * lax.axis_size("frame") * lax.axis_size("band")
    gs, gt = unpack(core, own, other, (9.0 * C) ** 0.5 / count, (3.0 * C) ** 0.5 / count)
    return gs.reshape(3, 3, C, C), gt


def solution(mesh):
    in_specs = (P("clip", "frame", "band", None, None), P(), P(), P(), P())
    return jax.shard_map(
        per_device, mesh=mesh, in_specs=in_specs, out_specs=(P(), P()), check_vma=False
    )
```

```python
import jax
import jax.numpy as jnp
from jax import lax
from jax.experimental import pallas as pl
from jax.experimental.pallas import tpu as pltpu
from jax.sharding import PartitionSpec as P

BF, F32 = jnp.bfloat16, jnp.float32
C = 320

RING = ("frame", "band")
UNIT = 152
FRAME_GROUPS = 8
ROWS = 64 * UNIT


def place(y, x, z):
    return (2 * y + x % 2) * 16 + 2 * z + x // 2


def ring_perm(axis, step):
    pairs = []
    for y in range(4):
        for x in range(4):
            for z in range(8):
                if axis == "x":
                    to = place(y, (x + step) % 4, z)
                elif axis == "y":
                    to = place((y + step) % 4, x, z)
                else:
                    to = place(y, x, (z + step) % 8)
                pairs.append((place(y, x, z), to))
    return pairs


def steps_of(count):
    order = []
    for s in range(1, count // 2):
        order += [s, -s]
    return [count // 2] + order[::-1]


def pick(parts, index):
    return lax.dynamic_index_in_dim(parts, index, 0, keepdims=False)


def send_scatter(parts, axis, at):
    count = parts.shape[0]
    return [
        lax.ppermute(pick(parts, (at + s) % count), RING, ring_perm(axis, s))
        for s in steps_of(count)
    ]


def send_gather(mine, axis, count):
    return [lax.ppermute(mine, RING, ring_perm(axis, s)) for s in steps_of(count)]


def arrange(mine, got, at):
    count = len(got) + 1
    whole = jnp.zeros((count,) + mine.shape, mine.dtype)
    whole = lax.dynamic_update_index_in_dim(whole, mine, at, 0)
    for s, piece in zip(steps_of(count), got):
        whole = lax.dynamic_update_index_in_dim(whole, piece, (at - s) % count, 0)
    return whole


def reduce_all(send, keep, ids):
    frame, band = ids[1], ids[2]
    y = frame // 2
    x = frame % 2 + 2 * (band % 2)
    z = band // 2
    swap = [(0, 1), (1, 0)]
    half = (keep + lax.ppermute(send, "clip", swap)).reshape(2, 4, 4, UNIT, 128)
    a, b = half[0], half[1]
    ga, gb = send_scatter(a, "x", x), send_scatter(b, "y", y)
    a = sum(ga, pick(a, x))
    b = sum(gb, pick(b, y))
    ga, gb = send_scatter(a, "y", y), send_scatter(b, "x", x)
    a = sum(ga, pick(a, y))
    b = sum(gb, pick(b, x))
    both = jnp.concatenate([a, b, jnp.zeros((16, 128), a.dtype)])
    parts = both.reshape(2, 160, 128)
    side = z & 1
    pair = [(place(y, x, z), place(y, x, z ^ 1)) for y in range(4) for x in range(4) for z in range(8)]
    both = pick(parts, side) + lax.ppermute(pick(parts, 1 - side), RING, pair)
    far, near, back = [lax.ppermute(both, RING, ring_perm("z", s)) for s in (4, 2, -2)]
    both = (both + far) + (near + back)
    other = lax.ppermute(both, RING, pair)
    low = side == 0
    both = jnp.concatenate([jnp.where(low, both, other), jnp.where(low, other, both)])
    a, b = both[:UNIT], both[UNIT : 2 * UNIT]
    ga, gb = send_gather(a, "y", 4), send_gather(b, "x", 4)
    a, b = arrange(a, ga, y), arrange(b, gb, x)
    ga, gb = send_gather(a, "x", 4), send_gather(b, "y", 4)
    a, b = arrange(a, ga, x), arrange(b, gb, y)
    half = jnp.stack([a, b])
    other = lax.ppermute(half, "clip", swap)
    return half.reshape(ROWS // 2, 128), other.reshape(ROWS // 2, 128)


def sds(shape, dtype):
    return jax.ShapeDtypeStruct(shape, dtype)


def cost(flops, nbytes):
    return pl.CostEstimate(flops=flops, transcendentals=0, bytes_accessed=nbytes)


def call(body, name, ins, outs, args, scratch=(), grant=16, flops=1000000000, through=(), alias=None):
    kinds = {"v": pltpu.VMEM, "h": pltpu.HBM, "s": pltpu.SMEM}
    args = [pltpu.with_memory_space_constraint(a, pltpu.HBM) if k == "h" else a for k, a in zip(ins, args)]
    alias = dict(alias or {})
    count = len(outs)
    outs = list(outs)
    for i in through:
        alias[i] = len(outs)
        outs.append((ins[i], sds(args[i].shape, args[i].dtype)))

    def inner_call(*refs):
        n = len(ins)
        body(*refs[: n + count], *refs[n + len(outs) :])

    return pl.pallas_call(
        inner_call,
        out_shape=tuple(pltpu.HBM(a.shape, a.dtype) if k == "h" else a for k, a in outs),
        in_specs=[pl.BlockSpec(memory_space=kinds[k]) for k in ins],
        out_specs=tuple(pl.BlockSpec(memory_space=kinds[k]) for k, _ in outs),
        input_output_aliases=alias,
        scratch_shapes=list(scratch),
        compiler_params=pltpu.CompilerParams(vmem_limit_bytes=grant << 20),
        cost_estimate=cost(flops, 1000000),
        name=name,
    )(*args)


def start(src, dst, sem):
    copy = pltpu.make_async_copy(src, dst, sem)
    copy.start()
    return copy


def dot(a, b):
    return jnp.dot(a, b, preferred_element_type=F32)


def dot_t(a, b):
    return lax.dot_general(a, b, (((0,), (0,)), ((), ())), preferred_element_type=F32)


def write_columns(row, out, at):
    wide = row.astype(F32)
    col = lax.broadcasted_iota(jnp.int32, (512, C), 0) & 63
    out[at, :, 0:C] = jnp.where(col == 0, 0.0, pltpu.roll(wide, 1, 0)).astype(BF)
    out[at, :, C : 2 * C] = row
    out[at, :, 2 * C : 3 * C] = jnp.where(col == 63, 0.0, pltpu.roll(wide, 511, 0)).astype(BF)


def edges_body(x_ref, ids_ref, down_ref, up_ref, same_ref, sem):
    for i in range(3):
        same_ref[i] = ids_ref[i]
    down = start(x_ref.at[:, 3], down_ref, sem.at[0])
    up = start(x_ref.at[:, 0], up_ref, sem.at[1])
    down.wait()
    up.wait()


def edges(x, ids):
    outs = [("v", sds((8, 64, C), BF))] * 2 + [("s", sds((3,), jnp.int32))]
    return call(edges_body, "edges", "hs", outs, (x, ids), (pltpu.SemaphoreType.DMA((2,)),), 4, 1000)


def inner_body(
    x_ref, sk_ref, st_ref, tk_ref, tt_ref,
    x6_ref, acc_ref, w_ref, tw_ref, tkt_ref,
    x_v, sk_v, st_v, tk_v, tt_v, sem,
):
    loads = [
        start(src, dst, sem.at[i])
        for i, (src, dst) in enumerate(
            ((x_ref, x_v), (sk_ref, sk_v), (st_ref, st_v), (tk_ref, tk_v), (tt_ref, tt_v))
        )
    ]
    tw_ref[C:384] = jnp.zeros((64, 3 * C), BF)
    tw_ref[384 + C : 768] = jnp.zeros((64, 3 * C), BF)
    loads[0].wait()

    def build(r, carry):
        write_columns(x_v[:, r].reshape(512, C), x6_ref, r + 1)
        return carry

    lax.fori_loop(0, 4, build, 0)
    for copy in loads[1:]:
        copy.wait()

    def lay(i, carry):
        w_ref[i, :, 0:C] = sk_v[i]
        w_ref[i, :, C:384] = jnp.zeros((3 * C, 64), BF)
        w_ref[i, :, 384 : 384 + C] = st_v[i]
        w_ref[i, :, 384 + C : 768] = jnp.zeros((3 * C, 64), BF)
        tkt_ref[pl.ds(pl.multiple_of(i * C, 64), C)] = tk_v[i].T
        return carry

    lax.fori_loop(0, 3, lay, 0)
    for k in range(3):
        tw_ref[0:C, k * C : (k + 1) * C] = tt_v[k]
        tw_ref[384 : 384 + C, k * C : (k + 1) * C] = tk_v[k]

    def taps(r, carry):
        acc_ref[r] = dot(x6_ref[r + 1], w_ref[1])

        @pl.when(r > 0)
        def _():
            acc_ref[r] += dot(x6_ref[r], w_ref[0])

        @pl.when(r < 3)
        def _():
            acc_ref[r] += dot(x6_ref[r + 2], w_ref[2])

        return carry

    lax.fori_loop(0, 4, taps, 0)


def inner(*args):
    outs = [
        ("v", sds((6, 512, 3 * C), BF)),
        ("v", sds((4, 512, 768), F32)),
        ("v", sds((3, 3 * C, 768), BF)),
        ("v", sds((768, 3 * C), BF)),
        ("v", sds((3 * C, C), BF)),
    ]
    scratch = (
        pltpu.VMEM((8, 4, 64, C), BF),
        pltpu.VMEM((3, 3 * C, C), BF),
        pltpu.VMEM((3, 3 * C, C), BF),
        pltpu.VMEM((3, C, C), BF),
        pltpu.VMEM((3, C, C), BF),
        pltpu.SemaphoreType.DMA((5,)),
    )
    return call(inner_body, "inner", "hhhhh", outs, args, scratch, 16, 6000000000)


def frame_rows(value, frame):
    return jnp.concatenate([value[frame * 64 : frame * 64 + 64], value[256 + frame * 64 : 320 + frame * 64]])


def outer_body(old_ref, top_ref, bot_ref, w_ref, acc_ref, tw_ref, tkt_ref, x6_ref, slope_ref, ad_ref, pn_ref, pp_ref, work_ref, rows_ref):
    rows_ref[0] = top_ref[...].reshape(512, C)
    rows_ref[1] = bot_ref[...].reshape(512, C)

    def build(e, carry):
        write_columns(rows_ref[e], x6_ref, 5 * e)
        work_ref[3 * e] = dot(x6_ref[5 * e], w_ref[2 * e])
        work_ref[1 + e] = jnp.zeros((512, 768), F32)
        return carry

    lax.fori_loop(0, 2, build, 0)

    def one(r, carry):
        hidden = acc_ref[r, :, 0:C] + work_ref[r, :, 0:C]
        tangent = acc_ref[r, :, 384 : 384 + C] + work_ref[r, :, 384 : 384 + C]
        sig = jax.nn.sigmoid(hidden)
        slope = sig * (1.0 + hidden * (1.0 - sig))
        slope_ref[r] = slope
        ad_ref[r, :, 0:C] = (hidden * sig).astype(BF)
        ad_ref[r, :, C:384] = jnp.zeros((512, 64), BF)
        ad_ref[r, :, 384 : 384 + C] = (slope * tangent).astype(BF)
        ad_ref[r, :, 384 + C : 768] = jnp.zeros((512, 64), BF)
        last = frame_rows(ad_ref[r], 3)
        first = frame_rows(ad_ref[r], 0)
        pn_ref[r] = dot(last, tw_ref[:, 0:C]).astype(BF)
        pp_ref[r] = dot(first, tw_ref[:, 2 * C : 3 * C]).astype(BF)
        return carry

    lax.fori_loop(0, 4, one, 0)


def outer(*args):
    outs = [
        ("v", sds((6, 512, 3 * C), BF)),
        ("v", sds((4, 512, C), F32)),
        ("v", sds((4, 512, 768), BF)),
        ("v", sds((4, 128, C), BF)),
        ("v", sds((4, 128, C), BF)),
    ]
    scratch = (pltpu.VMEM((4, 512, 768), F32), pltpu.VMEM((2, 512, C), BF))
    return call(outer_body, "outer", "vvvvvvv", outs, args, scratch, 16, 1500000000, (5, 6), {0: 0})


def own_res_body(ad_ref, tw_ref, x6_ref, slope_ref, tkt_ref, res_ref, first_ref, last_ref, u_ref):
    def one(r, carry):
        u_ref[...] = dot(ad_ref[r], tw_ref[...])
        for clip in range(2):
            o = 256 * clip
            res_ref[r, o : o + 256] = u_ref[o : o + 256, C : 2 * C]
            res_ref[r, o + 64 : o + 256] += u_ref[o : o + 192, 0:C]
            res_ref[r, o : o + 192] += u_ref[o + 64 : o + 256, 2 * C : 3 * C]
            first_ref[r, 64 * clip : 64 * clip + 64] = res_ref[r, o : o + 64].astype(BF)
            last_ref[r, 64 * clip : 64 * clip + 64] = res_ref[r, o + 192 : o + 256].astype(BF)
        return carry

    lax.fori_loop(0, 4, one, 0)


def own_res(*args):
    outs = [("v", sds((4, 512, C), F32)), ("v", sds((4, 128, C), BF)), ("v", sds((4, 128, C), BF))]
    scratch = (pltpu.VMEM((512, 3 * C), F32),)
    return call(own_res_body, "own_res", "vvvvv", outs, args, scratch, through=(0, 2, 3, 4))


def close_body(part_ref, before_ref, after_ref, ad_ref, x6_ref, slope_ref, tkt_ref, first_ref, last_ref):
    for clip in range(2):
        o, h = 256 * clip, 64 * clip
        edge = slice(h, h + 64)
        first_ref[:, edge] = (part_ref[:, o : o + 64] + before_ref[:, edge].astype(F32)).astype(BF)
        last_ref[:, edge] = (part_ref[:, o + 192 : o + 256] + after_ref[:, edge].astype(F32)).astype(BF)


def close(*args):
    outs = [("v", sds((4, 128, C), BF))] * 2
    return call(close_body, "close", "vvvvvvv", outs, args, (), 8, 1000000, (0, 3, 4, 5, 6))


def own_back_body(part_ref, first_ref, last_ref, ad_ref, x6_ref, slope_ref, tkt_ref, back_ref, gt_ref, r3_ref):
    gap = jnp.zeros((64, C), BF)

    def one(r, carry):
        for clip in range(2):
            o, h = 256 * clip, 64 * clip
            value = jnp.concatenate(
                [first_ref[r, h : h + 64], part_ref[r, o + 64 : o + 192].astype(BF), last_ref[r, h : h + 64]]
            )
            r3_ref[r, o : o + 192, 0:C] = value[64:256]
            r3_ref[r, o + 192 : o + 256, 0:C] = gap
            r3_ref[r, o : o + 256, C : 2 * C] = value
            r3_ref[r, o : o + 64, 2 * C : 3 * C] = gap
            r3_ref[r, o + 64 : o + 256, 2 * C : 3 * C] = value[0:192]
        back_ref[r] = dot(r3_ref[r], tkt_ref[...])
        return carry

    lax.fori_loop(0, 4, one, 0)
    gt_ref[...] = dot_t(ad_ref[:, :, 0:C].reshape(2048, C), r3_ref[...].reshape(2048, 3 * C))


def own_back(*args):
    outs = [("v", sds((4, 512, C), F32)), ("v", sds((C, 3 * C), F32))]
    scratch = (pltpu.VMEM((4, 512, 3 * C), BF),)
    return call(own_back_body, "own_back", "vvvvvvv", outs, args, scratch, through=(3, 4, 5, 6))


def put_columns(out_ref, start, value):
    done = 0
    while done < value.shape[1]:
        j, lane = (start + done) // 128, (start + done) % 128
        n = min(128 - lane, value.shape[1] - done)
        out_ref[j * C : (j + 1) * C, lane : lane + n] = value[:, done : done + n]
        done += n


def half_grads(which, hbt_ref, x6_ref, gt_ref, out_ref, turn):
    def one(n, carry):
        tap = 2 * which + n

        @pl.when(tap < 3)
        def _():
            turn[...] = dot(hbt_ref[...], x6_ref[pl.ds(tap, 4)].reshape(2048, 3 * C))

        @pl.when(tap == 3)
        def _():
            turn[...] = gt_ref[...]

        @pl.when(n == 0)
        def _():
            put_columns(out_ref, 0, turn[...])

        @pl.when(n == 1)
        def _():
            put_columns(out_ref, 3 * C, turn[...])

        return carry

    lax.fori_loop(0, 2, one, 0)
    out_ref[15 * C : ROWS // 2] = jnp.zeros((ROWS // 2 - 15 * C, 128), F32)


def send_body(core_ref, before_ref, after_ref, pn_ref, pp_ref, back_ref, slope_ref, ad_ref, tkt_ref, gt_ref, x6_ref, out_ref, hbt_ref, all_ref, hb_ref, halo_ref, turn):
    frame = core_ref[1]
    before = before_ref[...].astype(F32) + pp_ref[...].astype(F32)
    before = jnp.where(frame > 0, before, 0.0).astype(BF).reshape(512, C)
    after = after_ref[...].astype(F32) + pn_ref[...].astype(F32)
    after = jnp.where(frame < FRAME_GROUPS - 1, after, 0.0).astype(BF).reshape(512, C)
    halo_ref[0] = dot(before, tkt_ref[2 * C : 3 * C]).reshape(4, 128, C)
    halo_ref[1] = dot(after, tkt_ref[0:C]).reshape(4, 128, C)
    for clip in range(2):
        o, h = 256 * clip, 64 * clip
        first, last = slice(o, o + 64), slice(o + 192, o + 256)
        mid, edge = slice(o + 64, o + 192), slice(h, h + 64)
        hb_ref[:, first] = (slope_ref[:, first] * (back_ref[:, first] + halo_ref[0, :, edge])).astype(BF)
        hb_ref[:, mid] = (slope_ref[:, mid] * back_ref[:, mid]).astype(BF)
        hb_ref[:, last] = (slope_ref[:, last] * (back_ref[:, last] + halo_ref[1, :, edge])).astype(BF)
    act_last = jnp.concatenate([frame_rows(ad_ref[r], 3)[:, 0:C] for r in range(4)])
    act_first = jnp.concatenate([frame_rows(ad_ref[r], 0)[:, 0:C] for r in range(4)])
    all_ref[:, 0:C] = gt_ref[:, 0:C] + dot_t(act_last, after)
    all_ref[:, C : 2 * C] = gt_ref[:, C : 2 * C]
    all_ref[:, 2 * C : 3 * C] = gt_ref[:, 2 * C : 3 * C] + dot_t(act_first, before)
    hbt_ref[...] = hb_ref[...].reshape(2048, C).T
    half_grads(1 - core_ref[0], hbt_ref, x6_ref, all_ref, out_ref, turn)


def grads_send(*args):
    outs = [("v", sds((ROWS // 2, 128), F32)), ("v", sds((C, 2048), BF)), ("v", sds((C, 3 * C), F32))]
    scratch = (
        pltpu.VMEM((4, 512, C), BF),
        pltpu.VMEM((2, 4, 128, C), F32),
        pltpu.VMEM((C, 3 * C), F32),
    )
    return call(send_body, "grads_send", "svvvvvvvvvv", outs, args, scratch, 16, 2500000000, (10,))


def keep_body(core_ref, hbt_ref, x6_ref, gt_ref, out_ref, same_ref, turn):
    for i in range(3):
        same_ref[i] = core_ref[i]
    half_grads(core_ref[0], hbt_ref, x6_ref, gt_ref, out_ref, turn)


def grads_keep(*args):
    outs = [("v", sds((ROWS // 2, 128), F32)), ("s", sds((3,), jnp.int32))]
    return call(keep_body, "grads_keep", "svvv", outs, args, (pltpu.VMEM((C, 3 * C), F32),), 16, 2500000000)


def block(j):
    at = j * C if j < 15 else ROWS // 2 + (j - 15) * C
    return slice(at, at + C)


def unpack(core, own, other, scale_s, scale_t):
    def body(core_ref, own_ref, other_ref, gs_ref, gt_ref, buf_ref):
        at = core_ref[0]
        half = ROWS // 2
        buf_ref[pl.ds(at * half, half)] = own_ref[...]
        buf_ref[pl.ds((1 - at) * half, half)] = other_ref[...]
        def one(j, carry):
            at = pl.multiple_of(j * C + jnp.where(j < 15, 0, ROWS // 2 - 15 * C), 8)
            gs_ref[pl.ds(pl.multiple_of(j * 128, 128), 128)] = buf_ref[pl.ds(at, C)].T * scale_s
            return carry

        lax.fori_loop(0, 22, one, 0, unroll=2)
        gs_ref[22 * 128 : 9 * C] = buf_ref[block(22)].T[0:64] * scale_s
        for k in range(3):
            done = 0
            while done < C:
                j, lane = ((9 + k) * C + done) // 128, ((9 + k) * C + done) % 128
                n = min(128 - lane, C - done)
                gt_ref[k, :, done : done + n] = buf_ref[block(j), lane : lane + n] * scale_t
                done += n

    return pl.pallas_call(
        body,
        out_shape=(sds((9 * C, C), F32), sds((3, C, C), F32)),
        compiler_params=pltpu.CompilerParams(vmem_limit_bytes=32 << 20),
        in_specs=[
            pl.BlockSpec(memory_space=pltpu.SMEM),
            pl.BlockSpec(memory_space=pltpu.VMEM),
            pl.BlockSpec(memory_space=pltpu.VMEM),
        ],
        scratch_shapes=[pltpu.VMEM((ROWS, 128), F32)],
        cost_estimate=cost(2000000, 10000000),
        name="unpack",
    )(core, own, other)


def to_next(value, axis):
    n = lax.axis_size(axis)
    return lax.ppermute(value, axis, [(i, i + 1) for i in range(n - 1)])


def to_prev(value, axis):
    n = lax.axis_size(axis)
    return lax.ppermute(value, axis, [(i + 1, i) for i in range(n - 1)])


def per_device(latents, spatial_kernel, temporal_kernel, spatial_tangent, temporal_tangent):
    x = latents.reshape(8, 4, 64, C)
    ids = jnp.stack([lax.axis_index(name).astype(jnp.int32) for name in ("clip", "frame", "band")])
    down, up, core = edges(x, ids)
    top, bot = to_next(down, "band"), to_prev(up, "band")
    x6, acc, w, tw, tkt = inner(
        x,
        spatial_kernel.reshape(3, 3 * C, C),
        spatial_tangent.reshape(3, 3 * C, C),
        temporal_kernel,
        temporal_tangent,
    )
    x6, slope, ad, p_next, p_prev, tw, tkt = outer(x6, top, bot, w, acc, tw, tkt)
    before, after = to_next(p_next, "frame"), to_prev(p_prev, "frame")
    part, first, last, ad, x6, slope, tkt = own_res(ad, tw, x6, slope, tkt)
    far_before, far_after = to_next(last, "frame"), to_prev(first, "frame")
    first, last, part, ad, x6, slope, tkt = close(part, before, after, ad, x6, slope, tkt)
    back, gt, ad, x6, slope, tkt = own_back(part, first, last, ad, x6, slope, tkt)
    send, hbt, gt, x6 = grads_send(
        core, far_before, far_after, p_next, p_prev, back, slope, ad, tkt, gt, x6
    )
    keep, ids = grads_keep(core, hbt, x6, gt)
    own, other = reduce_all(send, keep, ids)
    count = 1.0 * latents.shape[0] * latents.shape[1] * latents.shape[2] * latents.shape[3]
    count = count * lax.axis_size("clip") * lax.axis_size("frame") * lax.axis_size("band")
    gs, gt = unpack(core, own, other, (9.0 * C) ** 0.5 / count, (3.0 * C) ** 0.5 / count)
    return gs.reshape(3, 3, C, C), gt


def solution(mesh):
    in_specs = (P("clip", "frame", "band", None, None), P(), P(), P(), P())
    return jax.shard_map(
        per_device, mesh=mesh, in_specs=in_specs, out_specs=(P(), P()), check_vma=False
    )
```

```python
import jax
import jax.numpy as jnp
from jax import lax
from jax.experimental import pallas as pl
from jax.experimental.pallas import tpu as pltpu
from jax.sharding import PartitionSpec as P

BF, F32 = jnp.bfloat16, jnp.float32
C = 320

RING = ("frame", "band")
UNIT = 152
FRAME_GROUPS = 8
ROWS = 64 * UNIT


def place(y, x, z):
    return (2 * y + x % 2) * 16 + 2 * z + x // 2


def ring_perm(axis, step):
    pairs = []
    for y in range(4):
        for x in range(4):
            for z in range(8):
                if axis == "x":
                    to = place(y, (x + step) % 4, z)
                elif axis == "y":
                    to = place((y + step) % 4, x, z)
                else:
                    to = place(y, x, (z + step) % 8)
                pairs.append((place(y, x, z), to))
    return pairs


def steps_of(count):
    order = []
    for s in range(1, count // 2):
        order += [s, -s]
    return [count // 2] + order[::-1]


def pick(parts, index):
    return lax.dynamic_index_in_dim(parts, index, 0, keepdims=False)


def send_scatter(parts, axis, at):
    count = parts.shape[0]
    return [
        lax.ppermute(pick(parts, (at + s % count) & (count - 1)), RING, ring_perm(axis, s))
        for s in steps_of(count)
    ]


def send_gather(mine, axis, count):
    return [lax.ppermute(mine, RING, ring_perm(axis, s)) for s in steps_of(count)]


def arrange(mine, got, at):
    count = len(got) + 1
    whole = jnp.zeros((count,) + mine.shape, mine.dtype)
    whole = lax.dynamic_update_index_in_dim(whole, mine, at, 0)
    for s, piece in zip(steps_of(count), got):
        whole = lax.dynamic_update_index_in_dim(whole, piece, (at + -s % count) & (count - 1), 0)
    return whole


def reduce_all(send, keep, ids):
    ids = ids.astype(jnp.uint32)
    frame, band = ids[1], ids[2]
    y = frame >> 1
    x = (frame & 1) + 2 * (band & 1)
    z = band >> 1
    swap = [(0, 1), (1, 0)]
    half = (keep + lax.ppermute(send, "clip", swap)).reshape(2, 4, 4, UNIT, 128)
    a, b = half[0], half[1]
    ga, gb = send_scatter(a, "x", x), send_scatter(b, "y", y)
    a = sum(ga, pick(a, x))
    b = sum(gb, pick(b, y))
    ga, gb = send_scatter(a, "y", y), send_scatter(b, "x", x)
    a = sum(ga, pick(a, y))
    b = sum(gb, pick(b, x))
    both = jnp.concatenate([a, b, jnp.zeros((16, 128), a.dtype)])
    parts = both.reshape(2, 160, 128)
    side = z & 1
    pair = [(place(y, x, z), place(y, x, z ^ 1)) for y in range(4) for x in range(4) for z in range(8)]
    both = pick(parts, side) + lax.ppermute(pick(parts, side ^ 1), RING, pair)
    far, near, back = [lax.ppermute(both, RING, ring_perm("z", s)) for s in (4, 2, -2)]
    both = (both + far) + (near + back)
    other = lax.ppermute(both, RING, pair)
    low = side == 0
    both = jnp.concatenate([jnp.where(low, both, other), jnp.where(low, other, both)])
    a, b = both[:UNIT], both[UNIT : 2 * UNIT]
    ga, gb = send_gather(a, "y", 4), send_gather(b, "x", 4)
    a, b = arrange(a, ga, y), arrange(b, gb, x)
    ga, gb = send_gather(a, "x", 4), send_gather(b, "y", 4)
    a, b = arrange(a, ga, x), arrange(b, gb, y)
    a, b = a.reshape(-1, 128), b.reshape(-1, 128)
    return a, b, lax.ppermute(a, "clip", swap), lax.ppermute(b, "clip", swap)


def sds(shape, dtype):
    return jax.ShapeDtypeStruct(shape, dtype)


def cost(flops, nbytes):
    return pl.CostEstimate(flops=flops, transcendentals=0, bytes_accessed=nbytes)


def call(body, name, ins, outs, args, scratch=(), grant=16, flops=1000000000, through=(), alias=None):
    kinds = {"v": pltpu.VMEM, "h": pltpu.HBM, "s": pltpu.SMEM}
    args = [pltpu.with_memory_space_constraint(a, pltpu.HBM) if k == "h" else a for k, a in zip(ins, args)]
    alias = dict(alias or {})
    count = len(outs)
    outs = list(outs)
    for i in through:
        alias[i] = len(outs)
        outs.append((ins[i], sds(args[i].shape, args[i].dtype)))

    def inner_call(*refs):
        n = len(ins)
        body(*refs[: n + count], *refs[n + len(outs) :])

    return pl.pallas_call(
        inner_call,
        out_shape=tuple(pltpu.HBM(a.shape, a.dtype) if k == "h" else a for k, a in outs),
        in_specs=[pl.BlockSpec(memory_space=kinds[k]) for k in ins],
        out_specs=tuple(pl.BlockSpec(memory_space=kinds[k]) for k, _ in outs),
        input_output_aliases=alias,
        scratch_shapes=list(scratch),
        compiler_params=pltpu.CompilerParams(vmem_limit_bytes=grant << 20),
        cost_estimate=cost(flops, 1000000),
        name=name,
    )(*args)


def start(src, dst, sem):
    copy = pltpu.make_async_copy(src, dst, sem)
    copy.start()
    return copy


def dot(a, b):
    return jnp.dot(a, b, preferred_element_type=F32)


def dot_t(a, b):
    return lax.dot_general(a, b, (((0,), (0,)), ((), ())), preferred_element_type=F32)


def write_columns(row, out, at):
    wide = row.astype(F32)
    col = lax.broadcasted_iota(jnp.int32, (512, C), 0) & 63
    out[at, :, 0:C] = jnp.where(col == 0, 0.0, pltpu.roll(wide, 1, 0)).astype(BF)
    out[at, :, C : 2 * C] = row
    out[at, :, 2 * C : 3 * C] = jnp.where(col == 63, 0.0, pltpu.roll(wide, 511, 0)).astype(BF)


def edges_body(x_ref, ids_ref, down_ref, up_ref, same_ref, sem):
    for i in range(3):
        same_ref[i] = ids_ref[i]
    down = start(x_ref.at[:, 3], down_ref, sem.at[0])
    up = start(x_ref.at[:, 0], up_ref, sem.at[1])
    down.wait()
    up.wait()


def edges(x, ids):
    outs = [("v", sds((8, 64, C), BF))] * 2 + [("s", sds((3,), jnp.int32))]
    return call(edges_body, "edges", "hs", outs, (x, ids), (pltpu.SemaphoreType.DMA((2,)),), 4, 1000)


def inner_body(
    x_ref, sk_ref, st_ref, tk_ref, tt_ref,
    x6_ref, acc_ref, w_ref, tw_ref, tkt_ref,
    x_v, sk_v, st_v, tk_v, tt_v, sem,
):
    loads = [
        start(src, dst, sem.at[i])
        for i, (src, dst) in enumerate(
            ((x_ref, x_v), (sk_ref, sk_v), (st_ref, st_v), (tk_ref, tk_v), (tt_ref, tt_v))
        )
    ]
    tw_ref[C:384] = jnp.zeros((64, 3 * C), BF)
    tw_ref[384 + C : 768] = jnp.zeros((64, 3 * C), BF)
    loads[0].wait()

    def build(r, carry):
        write_columns(x_v[:, r].reshape(512, C), x6_ref, r + 1)
        return carry

    lax.fori_loop(0, 4, build, 0)
    for copy in loads[1:]:
        copy.wait()

    def lay(i, carry):
        w_ref[i, :, 0:C] = sk_v[i]
        w_ref[i, :, C:384] = jnp.zeros((3 * C, 64), BF)
        w_ref[i, :, 384 : 384 + C] = st_v[i]
        w_ref[i, :, 384 + C : 768] = jnp.zeros((3 * C, 64), BF)
        tkt_ref[pl.ds(pl.multiple_of(i * C, 64), C)] = tk_v[i].T
        return carry

    lax.fori_loop(0, 3, lay, 0)
    for k in range(3):
        tw_ref[0:C, k * C : (k + 1) * C] = tt_v[k]
        tw_ref[384 : 384 + C, k * C : (k + 1) * C] = tk_v[k]

    def taps(r, carry):
        acc_ref[r] = jnp.zeros((512, 768), F32)

        def tap(i, inner_carry):
            @pl.when((r + i > 0) & (r + i < 5))
            def _():
                acc_ref[r] += dot(x6_ref[r + i], w_ref[i])

            return inner_carry

        return lax.fori_loop(0, 3, tap, carry)

    lax.fori_loop(0, 4, taps, 0)


def inner(*args):
    outs = [
        ("v", sds((6, 512, 3 * C), BF)),
        ("v", sds((4, 512, 768), F32)),
        ("v", sds((3, 3 * C, 768), BF)),
        ("v", sds((768, 3 * C), BF)),
        ("v", sds((3 * C, C), BF)),
    ]
    scratch = (
        pltpu.VMEM((8, 4, 64, C), BF),
        pltpu.VMEM((3, 3 * C, C), BF),
        pltpu.VMEM((3, 3 * C, C), BF),
        pltpu.VMEM((3, C, C), BF),
        pltpu.VMEM((3, C, C), BF),
        pltpu.SemaphoreType.DMA((5,)),
    )
    return call(inner_body, "inner", "hhhhh", outs, args, scratch, 16, 6000000000)


def frame_rows(value, frame):
    return jnp.concatenate([value[frame * 64 : frame * 64 + 64], value[256 + frame * 64 : 320 + frame * 64]])


def outer_body(old_ref, top_ref, bot_ref, w_ref, acc_ref, tw_ref, tkt_ref, x6_ref, slope_ref, ad_ref, pn_ref, pp_ref, work_ref, rows_ref):
    rows_ref[0] = top_ref[...].reshape(512, C)
    rows_ref[1] = bot_ref[...].reshape(512, C)

    def build(e, carry):
        write_columns(rows_ref[e], x6_ref, 5 * e)
        work_ref[3 * e] = dot(x6_ref[5 * e], w_ref[2 * e])
        work_ref[1 + e] = jnp.zeros((512, 768), F32)
        return carry

    lax.fori_loop(0, 2, build, 0)

    def one(r, carry):
        hidden = acc_ref[r, :, 0:C] + work_ref[r, :, 0:C]
        tangent = acc_ref[r, :, 384 : 384 + C] + work_ref[r, :, 384 : 384 + C]
        sig = jax.nn.sigmoid(hidden)
        slope = sig * (1.0 + hidden * (1.0 - sig))
        slope_ref[r] = slope
        ad_ref[r, :, 0:C] = (hidden * sig).astype(BF)
        ad_ref[r, :, C:384] = jnp.zeros((512, 64), BF)
        ad_ref[r, :, 384 : 384 + C] = (slope * tangent).astype(BF)
        ad_ref[r, :, 384 + C : 768] = jnp.zeros((512, 64), BF)
        last = frame_rows(ad_ref[r], 3)
        first = frame_rows(ad_ref[r], 0)
        pn_ref[r] = dot(last, tw_ref[:, 0:C]).astype(BF)
        pp_ref[r] = dot(first, tw_ref[:, 2 * C : 3 * C]).astype(BF)
        return carry

    lax.fori_loop(0, 4, one, 0)


def outer(*args):
    outs = [
        ("v", sds((6, 512, 3 * C), BF)),
        ("v", sds((4, 512, C), F32)),
        ("v", sds((4, 512, 768), BF)),
        ("v", sds((4, 128, C), BF)),
        ("v", sds((4, 128, C), BF)),
    ]
    scratch = (pltpu.VMEM((4, 512, 768), F32), pltpu.VMEM((2, 512, C), BF))
    return call(outer_body, "outer", "vvvvvvv", outs, args, scratch, 16, 1500000000, (5, 6), {0: 0})


def own_res_body(ad_ref, tw_ref, x6_ref, slope_ref, tkt_ref, res_ref, first_ref, last_ref, u_ref):
    def one(r, carry):
        u_ref[...] = dot(ad_ref[r], tw_ref[...])
        for clip in range(2):
            o = 256 * clip
            res_ref[r, o : o + 256] = u_ref[o : o + 256, C : 2 * C]
            res_ref[r, o + 64 : o + 256] += u_ref[o : o + 192, 0:C]
            res_ref[r, o : o + 192] += u_ref[o + 64 : o + 256, 2 * C : 3 * C]
            first_ref[r, 64 * clip : 64 * clip + 64] = res_ref[r, o : o + 64].astype(BF)
            last_ref[r, 64 * clip : 64 * clip + 64] = res_ref[r, o + 192 : o + 256].astype(BF)
        return carry

    lax.fori_loop(0, 4, one, 0)


def own_res(*args):
    outs = [("v", sds((4, 512, C), F32)), ("v", sds((4, 128, C), BF)), ("v", sds((4, 128, C), BF))]
    scratch = (pltpu.VMEM((512, 3 * C), F32),)
    return call(own_res_body, "own_res", "vvvvv", outs, args, scratch, through=(0, 2, 3, 4))


def close_body(part_ref, before_ref, after_ref, ad_ref, x6_ref, slope_ref, tkt_ref, first_ref, last_ref):
    for clip in range(2):
        o, h = 256 * clip, 64 * clip
        edge = slice(h, h + 64)
        first_ref[:, edge] = (part_ref[:, o : o + 64] + before_ref[:, edge].astype(F32)).astype(BF)
        last_ref[:, edge] = (part_ref[:, o + 192 : o + 256] + after_ref[:, edge].astype(F32)).astype(BF)


def close(*args):
    outs = [("v", sds((4, 128, C), BF))] * 2
    return call(close_body, "close", "vvvvvvv", outs, args, (), 8, 1000000, (0, 3, 4, 5, 6))


def own_back_body(part_ref, first_ref, last_ref, ad_ref, x6_ref, slope_ref, tkt_ref, back_ref, gt_ref, r3_ref):
    gap = jnp.zeros((64, C), BF)

    def one(r, carry):
        for clip in range(2):
            o, h = 256 * clip, 64 * clip
            value = jnp.concatenate(
                [first_ref[r, h : h + 64], part_ref[r, o + 64 : o + 192].astype(BF), last_ref[r, h : h + 64]]
            )
            r3_ref[r, o : o + 192, 0:C] = value[64:256]
            r3_ref[r, o + 192 : o + 256, 0:C] = gap
            r3_ref[r, o : o + 256, C : 2 * C] = value
            r3_ref[r, o : o + 64, 2 * C : 3 * C] = gap
            r3_ref[r, o + 64 : o + 256, 2 * C : 3 * C] = value[0:192]
        back_ref[r] = dot(r3_ref[r], tkt_ref[...])
        return carry

    lax.fori_loop(0, 4, one, 0)
    gt_ref[...] = dot_t(ad_ref[:, :, 0:C].reshape(2048, C), r3_ref[...].reshape(2048, 3 * C))


def own_back(*args):
    outs = [("v", sds((4, 512, C), F32)), ("v", sds((C, 3 * C), F32))]
    scratch = (pltpu.VMEM((4, 512, 3 * C), BF),)
    return call(own_back_body, "own_back", "vvvvvvv", outs, args, scratch, through=(3, 4, 5, 6))


def put_columns(out_ref, start, value):
    done = 0
    while done < value.shape[1]:
        j, lane = (start + done) // 128, (start + done) % 128
        n = min(128 - lane, value.shape[1] - done)
        out_ref[j * C : (j + 1) * C, lane : lane + n] = value[:, done : done + n]
        done += n


def half_grads(which, hbt_ref, x6_ref, gt_ref, out_ref, turn):
    def one(n, carry):
        tap = 2 * which + n

        @pl.when(tap < 3)
        def _():
            turn[...] = dot(hbt_ref[...], x6_ref[pl.ds(tap, 4)].reshape(2048, 3 * C))

        @pl.when(tap == 3)
        def _():
            turn[...] = gt_ref[...]

        @pl.when(n == 0)
        def _():
            put_columns(out_ref, 0, turn[...])

        @pl.when(n == 1)
        def _():
            put_columns(out_ref, 3 * C, turn[...])

        return carry

    lax.fori_loop(0, 2, one, 0)
    out_ref[15 * C : ROWS // 2] = jnp.zeros((ROWS // 2 - 15 * C, 128), F32)


def send_body(core_ref, before_ref, after_ref, pn_ref, pp_ref, back_ref, slope_ref, ad_ref, tkt_ref, gt_ref, x6_ref, out_ref, hbt_ref, all_ref, hb_ref, halo_ref, turn):
    frame = core_ref[1]
    before = before_ref[...].astype(F32) + pp_ref[...].astype(F32)
    before = jnp.where(frame > 0, before, 0.0).astype(BF).reshape(512, C)
    after = after_ref[...].astype(F32) + pn_ref[...].astype(F32)
    after = jnp.where(frame < FRAME_GROUPS - 1, after, 0.0).astype(BF).reshape(512, C)
    halo_ref[0] = dot(before, tkt_ref[2 * C : 3 * C]).reshape(4, 128, C)
    halo_ref[1] = dot(after, tkt_ref[0:C]).reshape(4, 128, C)
    for clip in range(2):
        o, h = 256 * clip, 64 * clip
        first, last = slice(o, o + 64), slice(o + 192, o + 256)
        mid, edge = slice(o + 64, o + 192), slice(h, h + 64)
        hb_ref[:, first] = (slope_ref[:, first] * (back_ref[:, first] + halo_ref[0, :, edge])).astype(BF)
        hb_ref[:, mid] = (slope_ref[:, mid] * back_ref[:, mid]).astype(BF)
        hb_ref[:, last] = (slope_ref[:, last] * (back_ref[:, last] + halo_ref[1, :, edge])).astype(BF)
    act_last = jnp.concatenate([frame_rows(ad_ref[r], 3)[:, 0:C] for r in range(4)])
    act_first = jnp.concatenate([frame_rows(ad_ref[r], 0)[:, 0:C] for r in range(4)])
    all_ref[:, 0:C] = gt_ref[:, 0:C] + dot_t(act_last, after)
    all_ref[:, C : 2 * C] = gt_ref[:, C : 2 * C]
    all_ref[:, 2 * C : 3 * C] = gt_ref[:, 2 * C : 3 * C] + dot_t(act_first, before)
    hbt_ref[...] = hb_ref[...].reshape(2048, C).T
    half_grads(1 - core_ref[0], hbt_ref, x6_ref, all_ref, out_ref, turn)


def grads_send(*args):
    outs = [("v", sds((ROWS // 2, 128), F32)), ("v", sds((C, 2048), BF)), ("v", sds((C, 3 * C), F32))]
    scratch = (
        pltpu.VMEM((4, 512, C), BF),
        pltpu.VMEM((2, 4, 128, C), F32),
        pltpu.VMEM((C, 3 * C), F32),
    )
    return call(send_body, "grads_send", "svvvvvvvvvv", outs, args, scratch, 16, 2500000000, (10,))


def keep_body(core_ref, hbt_ref, x6_ref, gt_ref, out_ref, same_ref, turn):
    for i in range(3):
        same_ref[i] = core_ref[i]
    half_grads(core_ref[0], hbt_ref, x6_ref, gt_ref, out_ref, turn)


def grads_keep(*args):
    outs = [("v", sds((ROWS // 2, 128), F32)), ("s", sds((3,), jnp.int32))]
    return call(keep_body, "grads_keep", "svvv", outs, args, (pltpu.VMEM((C, 3 * C), F32),), 16, 2500000000)


def block(j):
    at = j * C if j < 15 else ROWS // 2 + (j - 15) * C
    return slice(at, at + C)


def unpack(core, parts, scale_s, scale_t):
    def body(core_ref, own_a, own_b, other_a, other_b, gs_ref, gt_ref, buf_ref):
        at = core_ref[0]
        half = ROWS // 2
        quarter = half // 2
        buf_ref[pl.ds(at * half, quarter)] = own_a[...]
        buf_ref[pl.ds(at * half + quarter, quarter)] = own_b[...]
        buf_ref[pl.ds((1 - at) * half, quarter)] = other_a[...]
        buf_ref[pl.ds((1 - at) * half + quarter, quarter)] = other_b[...]
        def one(j, carry):
            at = pl.multiple_of(j * C + jnp.where(j < 15, 0, ROWS // 2 - 15 * C), 8)
            gs_ref[pl.ds(pl.multiple_of(j * 128, 128), 128)] = buf_ref[pl.ds(at, C)].T * scale_s
            return carry

        lax.fori_loop(0, 22, one, 0, unroll=2)
        gs_ref[22 * 128 : 9 * C] = buf_ref[block(22)].T[0:64] * scale_s
        for k in range(3):
            done = 0
            while done < C:
                j, lane = ((9 + k) * C + done) // 128, ((9 + k) * C + done) % 128
                n = min(128 - lane, C - done)
                gt_ref[k, :, done : done + n] = buf_ref[block(j), lane : lane + n] * scale_t
                done += n

    return pl.pallas_call(
        body,
        out_shape=(sds((9 * C, C), F32), sds((3, C, C), F32)),
        compiler_params=pltpu.CompilerParams(vmem_limit_bytes=32 << 20),
        in_specs=[
            pl.BlockSpec(memory_space=pltpu.SMEM),
        ]
        + [pl.BlockSpec(memory_space=pltpu.VMEM)] * 4,
        scratch_shapes=[pltpu.VMEM((ROWS, 128), F32)],
        cost_estimate=cost(2000000, 10000000),
        name="unpack",
    )(core, *parts)


def to_next(value, axis):
    n = lax.axis_size(axis)
    return lax.ppermute(value, axis, [(i, i + 1) for i in range(n - 1)])


def to_prev(value, axis):
    n = lax.axis_size(axis)
    return lax.ppermute(value, axis, [(i + 1, i) for i in range(n - 1)])


def per_device(latents, spatial_kernel, temporal_kernel, spatial_tangent, temporal_tangent):
    x = latents.reshape(8, 4, 64, C)
    ids = jnp.stack([lax.axis_index(name).astype(jnp.int32) for name in ("clip", "frame", "band")])
    down, up, core = edges(x, ids)
    top, bot = to_next(down, "band"), to_prev(up, "band")
    x6, acc, w, tw, tkt = inner(
        x,
        spatial_kernel.reshape(3, 3 * C, C),
        spatial_tangent.reshape(3, 3 * C, C),
        temporal_kernel,
        temporal_tangent,
    )
    x6, slope, ad, p_next, p_prev, tw, tkt = outer(x6, top, bot, w, acc, tw, tkt)
    before, after = to_next(p_next, "frame"), to_prev(p_prev, "frame")
    part, first, last, ad, x6, slope, tkt = own_res(ad, tw, x6, slope, tkt)
    far_before, far_after = to_next(last, "frame"), to_prev(first, "frame")
    first, last, part, ad, x6, slope, tkt = close(part, before, after, ad, x6, slope, tkt)
    back, gt, ad, x6, slope, tkt = own_back(part, first, last, ad, x6, slope, tkt)
    send, hbt, gt, x6 = grads_send(
        core, far_before, far_after, p_next, p_prev, back, slope, ad, tkt, gt, x6
    )
    keep, ids = grads_keep(core, hbt, x6, gt)
    parts = reduce_all(send, keep, ids)
    count = 1.0 * latents.shape[0] * latents.shape[1] * latents.shape[2] * latents.shape[3]
    count = count * lax.axis_size("clip") * lax.axis_size("frame") * lax.axis_size("band")
    gs, gt = unpack(core, parts, (9.0 * C) ** 0.5 / count, (3.0 * C) ** 0.5 / count)
    return gs.reshape(3, 3, C, C), gt


def solution(mesh):
    in_specs = (P("clip", "frame", "band", None, None), P(), P(), P(), P())
    return jax.shard_map(
        per_device, mesh=mesh, in_specs=in_specs, out_specs=(P(), P()), check_vma=False
    )
```

```python
import jax
import jax.numpy as jnp
from jax import lax
from jax.experimental import pallas as pl
from jax.experimental.pallas import tpu as pltpu
from jax.sharding import PartitionSpec as P

BF, F32 = jnp.bfloat16, jnp.float32
C = 320

RING = ("frame", "band")
UNIT = 152
FRAME_GROUPS = 8
ROWS = 64 * UNIT


def place(y, x, z):
    return (2 * y + x % 2) * 16 + 2 * z + x // 2


def ring_perm(axis, step):
    pairs = []
    for y in range(4):
        for x in range(4):
            for z in range(8):
                if axis == "x":
                    to = place(y, (x + step) % 4, z)
                elif axis == "y":
                    to = place((y + step) % 4, x, z)
                else:
                    to = place(y, x, (z + step) % 8)
                pairs.append((place(y, x, z), to))
    return pairs


def steps_of(count):
    order = []
    for s in range(1, count // 2):
        order += [s, -s]
    return [count // 2] + order[::-1]


def pick(parts, index):
    return lax.dynamic_index_in_dim(parts, index, 0, keepdims=False)


def send_scatter(parts, axis, at):
    count = parts.shape[0]
    return [
        lax.ppermute(pick(parts, (at + s % count) & (count - 1)), RING, ring_perm(axis, s))
        for s in steps_of(count)
    ]


def send_gather(mine, axis, count):
    return [lax.ppermute(mine, RING, ring_perm(axis, s)) for s in steps_of(count)]


def arrange(mine, got, at):
    count = len(got) + 1
    whole = jnp.zeros((count,) + mine.shape, mine.dtype)
    whole = lax.dynamic_update_index_in_dim(whole, mine, at, 0)
    for s, piece in zip(steps_of(count), got):
        whole = lax.dynamic_update_index_in_dim(whole, piece, (at + -s % count) & (count - 1), 0)
    return whole


def reduce_all(send, keep, ids):
    ids = ids.astype(jnp.uint32)
    frame, band = ids[1], ids[2]
    y = frame >> 1
    x = (frame & 1) + 2 * (band & 1)
    z = band >> 1
    swap = [(0, 1), (1, 0)]
    half = (keep + lax.ppermute(send, "clip", swap)).reshape(2, 4, 4, UNIT, 128)
    a, b = half[0], half[1]
    ga, gb = send_scatter(a, "x", x), send_scatter(b, "y", y)
    a = sum(ga, pick(a, x))
    b = sum(gb, pick(b, y))
    ga, gb = send_scatter(a, "y", y), send_scatter(b, "x", x)
    a = sum(ga, pick(a, y))
    b = sum(gb, pick(b, x))
    both = jnp.concatenate([a, b, jnp.zeros((16, 128), a.dtype)])
    parts = both.reshape(2, 160, 128)
    side = z & 1
    pair = [(place(y, x, z), place(y, x, z ^ 1)) for y in range(4) for x in range(4) for z in range(8)]
    both = pick(parts, side) + lax.ppermute(pick(parts, side ^ 1), RING, pair)
    far, near, back = [lax.ppermute(both, RING, ring_perm("z", s)) for s in (4, 2, -2)]
    both = (both + far) + (near + back)
    other = lax.ppermute(both, RING, pair)
    low = side == 0
    both = jnp.concatenate([jnp.where(low, both, other), jnp.where(low, other, both)])
    a, b = both[:UNIT], both[UNIT : 2 * UNIT]
    ga, gb = send_gather(a, "y", 4), send_gather(b, "x", 4)
    a, b = arrange(a, ga, y), arrange(b, gb, x)
    ga, gb = send_gather(a, "x", 4), send_gather(b, "y", 4)
    a, b = arrange(a, ga, x), arrange(b, gb, y)
    a, b = a.reshape(-1, 128), b.reshape(-1, 128)
    return a, b, lax.ppermute(a, "clip", swap), lax.ppermute(b, "clip", swap)


def sds(shape, dtype):
    return jax.ShapeDtypeStruct(shape, dtype)


def cost(flops, nbytes):
    return pl.CostEstimate(flops=flops, transcendentals=0, bytes_accessed=nbytes)


def call(body, name, ins, outs, args, scratch=(), grant=16, flops=1000000000, through=(), alias=None):
    kinds = {"v": pltpu.VMEM, "h": pltpu.HBM, "s": pltpu.SMEM}
    args = [pltpu.with_memory_space_constraint(a, pltpu.HBM) if k == "h" else a for k, a in zip(ins, args)]
    alias = dict(alias or {})
    count = len(outs)
    outs = list(outs)
    for i in through:
        alias[i] = len(outs)
        outs.append((ins[i], sds(args[i].shape, args[i].dtype)))

    def inner_call(*refs):
        n = len(ins)
        body(*refs[: n + count], *refs[n + len(outs) :])

    return pl.pallas_call(
        inner_call,
        out_shape=tuple(pltpu.HBM(a.shape, a.dtype) if k == "h" else a for k, a in outs),
        in_specs=[pl.BlockSpec(memory_space=kinds[k]) for k in ins],
        out_specs=tuple(pl.BlockSpec(memory_space=kinds[k]) for k, _ in outs),
        input_output_aliases=alias,
        scratch_shapes=list(scratch),
        compiler_params=pltpu.CompilerParams(vmem_limit_bytes=grant << 20),
        cost_estimate=cost(flops, 1000000),
        name=name,
    )(*args)


def start(src, dst, sem):
    copy = pltpu.make_async_copy(src, dst, sem)
    copy.start()
    return copy


def dot(a, b):
    return jnp.dot(a, b, preferred_element_type=F32)


def dot_t(a, b):
    return lax.dot_general(a, b, (((0,), (0,)), ((), ())), preferred_element_type=F32)


def write_columns(row, out, at):
    wide = row.astype(F32)
    col = lax.broadcasted_iota(jnp.int32, (512, C), 0) & 63
    out[at, :, 0:C] = jnp.where(col == 0, 0.0, pltpu.roll(wide, 1, 0)).astype(BF)
    out[at, :, C : 2 * C] = row
    out[at, :, 2 * C : 3 * C] = jnp.where(col == 63, 0.0, pltpu.roll(wide, 511, 0)).astype(BF)


def edges_body(x_ref, ids_ref, down_ref, up_ref, same_ref, sem):
    for i in range(3):
        same_ref[i] = ids_ref[i]
    down = start(x_ref.at[:, 3], down_ref, sem.at[0])
    up = start(x_ref.at[:, 0], up_ref, sem.at[1])
    down.wait()
    up.wait()


def edges(x, ids):
    outs = [("v", sds((8, 64, C), BF))] * 2 + [("s", sds((3,), jnp.int32))]
    return call(edges_body, "edges", "hs", outs, (x, ids), (pltpu.SemaphoreType.DMA((2,)),), 4, 1000)


def inner_body(
    x_ref, sk_ref, st_ref, tk_ref, tt_ref,
    x6_ref, acc_ref, w_ref, tw_ref, tkt_ref,
    x_v, sk_v, st_v, tk_v, tt_v, sem,
):
    loads = [
        start(src, dst, sem.at[i])
        for i, (src, dst) in enumerate(
            ((x_ref, x_v), (sk_ref, sk_v), (st_ref, st_v), (tk_ref, tk_v), (tt_ref, tt_v))
        )
    ]
    tw_ref[C:384] = jnp.zeros((64, 3 * C), BF)
    tw_ref[384 + C : 768] = jnp.zeros((64, 3 * C), BF)
    loads[0].wait()

    def build(r, carry):
        write_columns(x_v[:, r].reshape(512, C), x6_ref, r + 1)
        return carry

    lax.fori_loop(0, 4, build, 0)
    for copy in loads[1:]:
        copy.wait()

    def lay(i, carry):
        w_ref[i, :, 0:C] = sk_v[i]
        w_ref[i, :, C:384] = jnp.zeros((3 * C, 64), BF)
        w_ref[i, :, 384 : 384 + C] = st_v[i]
        w_ref[i, :, 384 + C : 768] = jnp.zeros((3 * C, 64), BF)
        tkt_ref[pl.ds(pl.multiple_of(i * C, 64), C)] = tk_v[i].T
        return carry

    lax.fori_loop(0, 3, lay, 0)
    for k in range(3):
        tw_ref[0:C, k * C : (k + 1) * C] = tt_v[k]
        tw_ref[384 : 384 + C, k * C : (k + 1) * C] = tk_v[k]

    def taps(r, carry):
        acc_ref[r] = jnp.zeros((512, 768), F32)

        def tap(i, inner_carry):
            @pl.when((r + i > 0) & (r + i < 5))
            def _():
                acc_ref[r] += dot(x6_ref[r + i], w_ref[i])

            return inner_carry

        return lax.fori_loop(0, 3, tap, carry)

    lax.fori_loop(0, 4, taps, 0)


def inner(*args):
    outs = [
        ("v", sds((6, 512, 3 * C), BF)),
        ("v", sds((4, 512, 768), F32)),
        ("v", sds((3, 3 * C, 768), BF)),
        ("v", sds((768, 3 * C), BF)),
        ("v", sds((3 * C, C), BF)),
    ]
    scratch = (
        pltpu.VMEM((8, 4, 64, C), BF),
        pltpu.VMEM((3, 3 * C, C), BF),
        pltpu.VMEM((3, 3 * C, C), BF),
        pltpu.VMEM((3, C, C), BF),
        pltpu.VMEM((3, C, C), BF),
        pltpu.SemaphoreType.DMA((5,)),
    )
    return call(inner_body, "inner", "hhhhh", outs, args, scratch, 16, 6000000000)


def frame_rows(value, frame):
    return jnp.concatenate([value[frame * 64 : frame * 64 + 64], value[256 + frame * 64 : 320 + frame * 64]])


def outer_body(old_ref, top_ref, bot_ref, w_ref, acc_ref, tw_ref, tkt_ref, x6_ref, slope_ref, ad_ref, pn_ref, pp_ref, work_ref, rows_ref):
    rows_ref[0] = top_ref[...].reshape(512, C)
    rows_ref[1] = bot_ref[...].reshape(512, C)

    def build(e, carry):
        write_columns(rows_ref[e], x6_ref, 5 * e)
        work_ref[3 * e] = dot(x6_ref[5 * e], w_ref[2 * e])
        work_ref[1 + e] = jnp.zeros((512, 768), F32)
        return carry

    lax.fori_loop(0, 2, build, 0)

    def one(r, carry):
        hidden = acc_ref[r, :, 0:C] + work_ref[r, :, 0:C]
        tangent = acc_ref[r, :, 384 : 384 + C] + work_ref[r, :, 384 : 384 + C]
        sig = jax.nn.sigmoid(hidden)
        slope = sig * (1.0 + hidden * (1.0 - sig))
        slope_ref[r] = slope
        ad_ref[r, :, 0:C] = (hidden * sig).astype(BF)
        ad_ref[r, :, C:384] = jnp.zeros((512, 64), BF)
        ad_ref[r, :, 384 : 384 + C] = (slope * tangent).astype(BF)
        ad_ref[r, :, 384 + C : 768] = jnp.zeros((512, 64), BF)
        last = frame_rows(ad_ref[r], 3)
        first = frame_rows(ad_ref[r], 0)
        pn_ref[r] = dot(last, tw_ref[:, 0:C]).astype(BF)
        pp_ref[r] = dot(first, tw_ref[:, 2 * C : 3 * C]).astype(BF)
        return carry

    lax.fori_loop(0, 4, one, 0)


def outer(*args):
    outs = [
        ("v", sds((6, 512, 3 * C), BF)),
        ("v", sds((4, 512, C), F32)),
        ("v", sds((4, 512, 768), BF)),
        ("v", sds((4, 128, C), BF)),
        ("v", sds((4, 128, C), BF)),
    ]
    scratch = (pltpu.VMEM((4, 512, 768), F32), pltpu.VMEM((2, 512, C), BF))
    return call(outer_body, "outer", "vvvvvvv", outs, args, scratch, 16, 1500000000, (5, 6), {0: 0})


def own_res_body(ad_ref, tw_ref, x6_ref, slope_ref, tkt_ref, res_ref, first_ref, last_ref, u_ref):
    def one(r, carry):
        u_ref[...] = dot(ad_ref[r], tw_ref[...])
        for clip in range(2):
            o = 256 * clip
            res_ref[r, o : o + 256] = u_ref[o : o + 256, C : 2 * C]
            res_ref[r, o + 64 : o + 256] += u_ref[o : o + 192, 0:C]
            res_ref[r, o : o + 192] += u_ref[o + 64 : o + 256, 2 * C : 3 * C]
            first_ref[r, 64 * clip : 64 * clip + 64] = res_ref[r, o : o + 64].astype(BF)
            last_ref[r, 64 * clip : 64 * clip + 64] = res_ref[r, o + 192 : o + 256].astype(BF)
        return carry

    lax.fori_loop(0, 4, one, 0)


def own_res(*args):
    outs = [("v", sds((4, 512, C), F32)), ("v", sds((4, 128, C), BF)), ("v", sds((4, 128, C), BF))]
    scratch = (pltpu.VMEM((512, 3 * C), F32),)
    return call(own_res_body, "own_res", "vvvvv", outs, args, scratch, through=(0, 2, 3, 4))


def close_body(part_ref, before_ref, after_ref, ad_ref, x6_ref, slope_ref, tkt_ref, first_ref, last_ref):
    for clip in range(2):
        o, h = 256 * clip, 64 * clip
        edge = slice(h, h + 64)
        first_ref[:, edge] = (part_ref[:, o : o + 64] + before_ref[:, edge].astype(F32)).astype(BF)
        last_ref[:, edge] = (part_ref[:, o + 192 : o + 256] + after_ref[:, edge].astype(F32)).astype(BF)


def close(*args):
    outs = [("v", sds((4, 128, C), BF))] * 2
    return call(close_body, "close", "vvvvvvv", outs, args, (), 8, 1000000, (0, 3, 4, 5, 6))


def own_back_body(part_ref, first_ref, last_ref, ad_ref, x6_ref, slope_ref, tkt_ref, back_ref, gt_ref, r3_ref):
    gap = jnp.zeros((64, C), BF)

    def one(r, carry):
        for clip in range(2):
            o, h = 256 * clip, 64 * clip
            value = jnp.concatenate(
                [first_ref[r, h : h + 64], part_ref[r, o + 64 : o + 192].astype(BF), last_ref[r, h : h + 64]]
            )
            r3_ref[r, o : o + 192, 0:C] = value[64:256]
            r3_ref[r, o + 192 : o + 256, 0:C] = gap
            r3_ref[r, o : o + 256, C : 2 * C] = value
            r3_ref[r, o : o + 64, 2 * C : 3 * C] = gap
            r3_ref[r, o + 64 : o + 256, 2 * C : 3 * C] = value[0:192]
        back_ref[r] = dot(r3_ref[r], tkt_ref[...])
        return carry

    lax.fori_loop(0, 4, one, 0)
    gt_ref[...] = dot_t(ad_ref[:, :, 0:C].reshape(2048, C), r3_ref[...].reshape(2048, 3 * C))


def own_back(*args):
    outs = [("v", sds((4, 512, C), F32)), ("v", sds((C, 3 * C), F32))]
    scratch = (pltpu.VMEM((4, 512, 3 * C), BF),)
    return call(own_back_body, "own_back", "vvvvvvv", outs, args, scratch, through=(3, 4, 5, 6))


def put_columns(out_ref, start, value):
    done = 0
    while done < value.shape[1]:
        j, lane = (start + done) // 128, (start + done) % 128
        n = min(128 - lane, value.shape[1] - done)
        out_ref[j * C : (j + 1) * C, lane : lane + n] = value[:, done : done + n]
        done += n


def half_grads(which, hbt_ref, x6_ref, gt_ref, out_ref, turn):
    def one(n, carry):
        tap = 2 * which + n

        @pl.when(tap < 3)
        def _():
            turn[...] = dot(hbt_ref[...], x6_ref[pl.ds(tap, 4)].reshape(2048, 3 * C))

        @pl.when(tap == 3)
        def _():
            turn[...] = gt_ref[...]

        @pl.when(n == 0)
        def _():
            put_columns(out_ref, 0, turn[...])

        @pl.when(n == 1)
        def _():
            put_columns(out_ref, 3 * C, turn[...])

        return carry

    lax.fori_loop(0, 2, one, 0)
    out_ref[15 * C : ROWS // 2] = jnp.zeros((ROWS // 2 - 15 * C, 128), F32)


def send_body(core_ref, before_ref, after_ref, pn_ref, pp_ref, back_ref, slope_ref, ad_ref, tkt_ref, gt_ref, x6_ref, out_ref, hbt_ref, all_ref, hb_ref, halo_ref, turn):
    frame = core_ref[1]
    before = before_ref[...].astype(F32) + pp_ref[...].astype(F32)
    before = jnp.where(frame > 0, before, 0.0).astype(BF).reshape(512, C)
    after = after_ref[...].astype(F32) + pn_ref[...].astype(F32)
    after = jnp.where(frame < FRAME_GROUPS - 1, after, 0.0).astype(BF).reshape(512, C)
    halo_ref[0] = dot(before, tkt_ref[2 * C : 3 * C]).reshape(4, 128, C)
    halo_ref[1] = dot(after, tkt_ref[0:C]).reshape(4, 128, C)
    for clip in range(2):
        o, h = 256 * clip, 64 * clip
        first, last = slice(o, o + 64), slice(o + 192, o + 256)
        mid, edge = slice(o + 64, o + 192), slice(h, h + 64)
        hb_ref[:, first] = (slope_ref[:, first] * (back_ref[:, first] + halo_ref[0, :, edge])).astype(BF)
        hb_ref[:, mid] = (slope_ref[:, mid] * back_ref[:, mid]).astype(BF)
        hb_ref[:, last] = (slope_ref[:, last] * (back_ref[:, last] + halo_ref[1, :, edge])).astype(BF)
    act_last = jnp.concatenate([frame_rows(ad_ref[r], 3)[:, 0:C] for r in range(4)])
    act_first = jnp.concatenate([frame_rows(ad_ref[r], 0)[:, 0:C] for r in range(4)])
    all_ref[:, 0:C] = gt_ref[:, 0:C] + dot_t(act_last, after)
    all_ref[:, C : 2 * C] = gt_ref[:, C : 2 * C]
    all_ref[:, 2 * C : 3 * C] = gt_ref[:, 2 * C : 3 * C] + dot_t(act_first, before)
    hbt_ref[...] = hb_ref[...].reshape(2048, C).T
    half_grads(1 - core_ref[0], hbt_ref, x6_ref, all_ref, out_ref, turn)


def grads_send(*args):
    outs = [("v", sds((ROWS // 2, 128), F32)), ("v", sds((C, 2048), BF)), ("v", sds((C, 3 * C), F32))]
    scratch = (
        pltpu.VMEM((4, 512, C), BF),
        pltpu.VMEM((2, 4, 128, C), F32),
        pltpu.VMEM((C, 3 * C), F32),
    )
    return call(send_body, "grads_send", "svvvvvvvvvv", outs, args, scratch, 16, 2500000000, (10,))


def keep_body(core_ref, hbt_ref, x6_ref, gt_ref, out_ref, same_ref, turn):
    for i in range(3):
        same_ref[i] = core_ref[i]
    half_grads(core_ref[0], hbt_ref, x6_ref, gt_ref, out_ref, turn)


def grads_keep(*args):
    outs = [("v", sds((ROWS // 2, 128), F32)), ("s", sds((3,), jnp.int32))]
    return call(keep_body, "grads_keep", "svvv", outs, args, (pltpu.VMEM((C, 3 * C), F32),), 16, 2500000000)


def block(j):
    at = j * C if j < 15 else ROWS // 2 + (j - 15) * C
    return slice(at, at + C)


def unpack(core, parts, scale_s, scale_t):
    def body(core_ref, own_a, own_b, other_a, other_b, gs_ref, gt_ref, buf_ref, gs_v, gt_v, sem):
        at = core_ref[0]
        half = ROWS // 2
        quarter = half // 2
        buf_ref[pl.ds(at * half, quarter)] = own_a[...]
        buf_ref[pl.ds(at * half + quarter, quarter)] = own_b[...]
        buf_ref[pl.ds((1 - at) * half, quarter)] = other_a[...]
        buf_ref[pl.ds((1 - at) * half + quarter, quarter)] = other_b[...]
        def block_copy(j):
            rows = pl.ds(pl.multiple_of(j * 128, 128), 128)
            return pltpu.make_async_copy(gs_v.at[rows], gs_ref.at[rows], sem.at[j])

        def one(j, carry):
            at = pl.multiple_of(j * C + jnp.where(j < 15, 0, ROWS // 2 - 15 * C), 8)
            gs_v[pl.ds(pl.multiple_of(j * 128, 128), 128)] = buf_ref[pl.ds(at, C)].T * scale_s
            block_copy(j).start()
            return carry

        lax.fori_loop(0, 22, one, 0, unroll=2)
        gs_v[22 * 128 : 9 * C] = buf_ref[block(22)].T[0:64] * scale_s
        tail = start(gs_v.at[22 * 128 : 9 * C], gs_ref.at[22 * 128 : 9 * C], sem.at[22])
        for k in range(3):
            done = 0
            while done < C:
                j, lane = ((9 + k) * C + done) // 128, ((9 + k) * C + done) % 128
                n = min(128 - lane, C - done)
                gt_v[k, :, done : done + n] = buf_ref[block(j), lane : lane + n] * scale_t
                done += n
        rest = start(gt_v, gt_ref, sem.at[23])

        def finish(j, carry):
            block_copy(j).wait()
            return carry

        lax.fori_loop(0, 22, finish, 0)
        tail.wait()
        rest.wait()

    return pl.pallas_call(
        body,
        out_shape=(pltpu.HBM((9 * C, C), F32), pltpu.HBM((3, C, C), F32)),
        out_specs=(pl.BlockSpec(memory_space=pltpu.HBM), pl.BlockSpec(memory_space=pltpu.HBM)),
        compiler_params=pltpu.CompilerParams(vmem_limit_bytes=32 << 20),
        in_specs=[
            pl.BlockSpec(memory_space=pltpu.SMEM),
        ]
        + [pl.BlockSpec(memory_space=pltpu.VMEM)] * 4,
        scratch_shapes=[
            pltpu.VMEM((ROWS, 128), F32),
            pltpu.VMEM((9 * C, C), F32),
            pltpu.VMEM((3, C, C), F32),
            pltpu.SemaphoreType.DMA((24,)),
        ],
        cost_estimate=cost(2000000, 10000000),
        name="unpack",
    )(core, *parts)


def to_next(value, axis):
    n = lax.axis_size(axis)
    return lax.ppermute(value, axis, [(i, i + 1) for i in range(n - 1)])


def to_prev(value, axis):
    n = lax.axis_size(axis)
    return lax.ppermute(value, axis, [(i + 1, i) for i in range(n - 1)])


def per_device(latents, spatial_kernel, temporal_kernel, spatial_tangent, temporal_tangent):
    x = latents.reshape(8, 4, 64, C)
    ids = jnp.stack([lax.axis_index(name).astype(jnp.int32) for name in ("clip", "frame", "band")])
    down, up, core = edges(x, ids)
    top, bot = to_next(down, "band"), to_prev(up, "band")
    x6, acc, w, tw, tkt = inner(
        x,
        spatial_kernel.reshape(3, 3 * C, C),
        spatial_tangent.reshape(3, 3 * C, C),
        temporal_kernel,
        temporal_tangent,
    )
    x6, slope, ad, p_next, p_prev, tw, tkt = outer(x6, top, bot, w, acc, tw, tkt)
    before, after = to_next(p_next, "frame"), to_prev(p_prev, "frame")
    part, first, last, ad, x6, slope, tkt = own_res(ad, tw, x6, slope, tkt)
    far_before, far_after = to_next(last, "frame"), to_prev(first, "frame")
    first, last, part, ad, x6, slope, tkt = close(part, before, after, ad, x6, slope, tkt)
    back, gt, ad, x6, slope, tkt = own_back(part, first, last, ad, x6, slope, tkt)
    send, hbt, gt, x6 = grads_send(
        core, far_before, far_after, p_next, p_prev, back, slope, ad, tkt, gt, x6
    )
    keep, ids = grads_keep(core, hbt, x6, gt)
    parts = reduce_all(send, keep, ids)
    count = 1.0 * latents.shape[0] * latents.shape[1] * latents.shape[2] * latents.shape[3]
    count = count * lax.axis_size("clip") * lax.axis_size("frame") * lax.axis_size("band")
    gs, gt = unpack(core, parts, (9.0 * C) ** 0.5 / count, (3.0 * C) ** 0.5 / count)
    return gs.reshape(3, 3, C, C), gt


def solution(mesh):
    in_specs = (P("clip", "frame", "band", None, None), P(), P(), P(), P())
    return jax.shard_map(
        per_device, mesh=mesh, in_specs=in_specs, out_specs=(P(), P()), check_vma=False
    )
```
